32 devices in a mesh: blk: 16 (over z, y, x), rhs: 2 (over core).
Axes of the slice: x: 2, y: 2, z: 4, core: 2. Of those that a mesh axis runs over, the one named last changes fastest.
Arguments:
- panel: int32 [1], replicated, may hold values from 0 to 19
- strips: bfloat16 [2, 6, 4096, 1024], P(None, None, 'blk'), may hold values from -0.078125 to 0.078125
- dinv_rows: bfloat16 [6, 4096, 1024], P(None, 'blk'), as said below
- fwd_state: float32 [6, 4096, 1024], P(None, 'blk', 'rhs'), may hold values from -6 to 6
- back_state: float32 [6, 4096, 1024], P(None, 'blk', 'rhs'), may hold values from -6 to 6
Outputs:
- fwd_out: float32 [6, 4096, 1024], P(None, 'blk', 'rhs')
- back_out: float32 [6, 4096, 1024], P(None, 'blk', 'rhs')
The draws below stay inside these ranges and needn't reach their ends.
Inputs may be any that keep to these rules, and one draw needn't show every extreme that they name: `dinv_rows`: E_k transposed is lower triangular, with its diagonal between 0.5 and 1.5.
All inputs are finite; a program needn't handle non-finite values.
Results may differ from the reference program's by a relative error of at most 0.0015.
Values may be sent and summed in bfloat16 or wider, within the bound.
No kernel may reach another device: no remote copies, remote signals or barrier semaphores. Data moves between devices by JAX's collectives and lax.ppermute only.
A program may use at most 64 MiB of HBM per device.

```python
import math
import jax
import jax.numpy as jnp
from jax import lax

PB = 1024
RHS = 1024
TPD = 6
LANE = 4096
NROWS = 24576
NPAN = 24


def draw_dinv_rows(key, part):
    first, second = jax.random.split(jax.random.fold_in(key, 7))
    inner = (jnp.arange(NROWS, dtype=jnp.int32) % PB)[:, None]
    column = jnp.arange(PB, dtype=jnp.int32)[None, :]
    diag = jax.random.uniform(first, (NROWS, 1), jnp.float32, 0.7, 1.3)
    noise = jax.random.normal(second, (NROWS, PB), jnp.float32) * 0.8 / math.sqrt(PB)
    full = jnp.where(column == inner, diag, jnp.where(column > inner, noise, 0.0))
    return full.reshape(TPD, LANE, PB).astype(jnp.bfloat16)


def block_levels(key, shape, shards, least, largest):
    level = 1.0
    for position, blocks in shards:
        heights = jax.random.uniform(jax.random.fold_in(jax.random.fold_in(key, 6), position), (blocks,), jnp.float32, least / len(shards), largest / len(shards))
        level = level * jnp.repeat(jnp.exp(heights), shape[position] // blocks).reshape((-1,) + (1,) * (len(shape) - 1 - position))
    return level


def centred(key, shape, spread, reach, cuts=(), kind=jnp.bfloat16):
    factor_of = block_levels(key, shape, cuts, -0.22, 0.18) if cuts else 1.0
    array = jax.random.normal(key, shape, jnp.float32) * spread * factor_of
    return jnp.minimum(jnp.maximum(array, -reach), reach).astype(kind)


def setup_inputs(seed: int = 0) -> dict:
    splits = jax.random.split(jax.random.key(seed), 6)
    panel = jax.random.randint(splits[0], (1,), 0, NPAN - LANE // PB).astype(jnp.int32)
    strips = centred(splits[1], (2, TPD, LANE, PB), (NROWS // 4) ** -0.5, 0.078125, ((2, 16),))
    dinv_rows = draw_dinv_rows(jax.random.fold_in(splits[5], 71), 0)
    fwd_state = centred(splits[3], (TPD, LANE, RHS), 1.0, 6.0, ((1, 16), (2, 2)), jnp.float32)
    back_state = centred(splits[4], (TPD, LANE, RHS), 1.0, 6.0, ((1, 16), (2, 2)), jnp.float32)
    return dict(panel=panel, strips=strips, dinv_rows=dinv_rows, fwd_state=fwd_state, back_state=back_state)


def reference(panel, strips, dinv_rows, fwd_state, back_state):
    rows_all = TPD * LANE
    lower = strips.reshape(2, rows_all, PB)
    inverse = dinv_rows.reshape(rows_all, PB)
    forward_rows = fwd_state.reshape(rows_all, RHS)
    backward_rows = back_state.reshape(rows_all, RHS)
    start = panel[0].astype(jnp.int32)
    block = (jnp.arange(rows_all, dtype=jnp.int32) // PB).astype(jnp.int32)

    def forward(k, which, state):
        head = (k * PB).astype(jnp.int32)
        current = lax.dynamic_slice_in_dim(state, head, PB, 0)
        block_inv = lax.dynamic_slice_in_dim(inverse, head, PB, 0)
        solved = lax.dot_general(block_inv, current.astype(jnp.bfloat16), (((0,), (0,)), ((), ())), preferred_element_type=jnp.float32)
        delta = jnp.dot(lower[which], solved.astype(jnp.bfloat16), preferred_element_type=jnp.float32)
        state = jnp.where((block > k)[:, None], state - delta, state)
        return lax.dynamic_update_slice_in_dim(state, solved, head, 0)

    def backward(k, which, state):
        head = (k * PB).astype(jnp.int32)
        current = lax.dynamic_slice_in_dim(state, head, PB, 0)
        block_inv = lax.dynamic_slice_in_dim(inverse, head, PB, 0)
        known = jnp.where((block > k)[:, None], state, 0.0).astype(jnp.bfloat16)
        summed = current - lax.dot_general(lower[which], known, (((0,), (0,)), ((), ())), preferred_element_type=jnp.float32)
        solved = jnp.dot(block_inv, summed.astype(jnp.bfloat16), preferred_element_type=jnp.float32)
        return lax.dynamic_update_slice_in_dim(state, solved, head, 0)

    forward_rows = forward(start, 0, forward_rows)
    forward_rows = forward(start + 1, 1, forward_rows)
    backward_rows = backward(start + 1, 1, backward_rows)
    backward_rows = backward(start, 0, backward_rows)
    return forward_rows.reshape(TPD, LANE, RHS), backward_rows.reshape(TPD, LANE, RHS)
```

```python
import functools

import jax
import jax.numpy as jnp
from jax import lax
from jax.experimental import pallas as pl
from jax.experimental.pallas import tpu as pltpu
from jax.sharding import PartitionSpec as P

BF = jnp.bfloat16
HF = jnp.float16
F32 = jnp.float32
SUM_SCALE = 4.0
VMEM = 100 * 1024 * 1024 // 2

NT = (((1,), (1,)), ((), ()))
NN = (((1,), (0,)), ((), ()))


def mm(a, b, dims):
    return lax.dot_general(a, b, dims, preferred_element_type=F32)


def plain_body(panel, strips, dinv_rows, fwd_state, back_state):
    tiles, span, columns = fwd_state.shape
    width = strips.shape[3]
    per_panel = width // span
    blocks = lax.axis_size("blk")
    device = lax.axis_index("blk")
    start = panel[0]
    slots = jnp.arange(tiles, dtype=jnp.int32)
    block_of = (slots * blocks + device) // per_panel

    def locate(k):
        offset = jnp.mod(device - per_panel * k, blocks)
        holds = offset < per_panel
        local = jnp.clip((per_panel * k + offset) // blocks, 0, tiles - 1)
        return (holds, local, jnp.minimum(offset, per_panel - 1))

    def forward(k, which, state):
        holds, local, offset = locate(k)
        strip = strips[which]
        current = lax.dynamic_index_in_dim(state, local, 0, keepdims=False).astype(BF)
        inv_tile = lax.dynamic_index_in_dim(dinv_rows, local, 0, keepdims=False)
        partial_rows = lax.dot_general(
            inv_tile, current, (((0,), (0,)), ((), ())), preferred_element_type=F32
        )
        partial_rows = jnp.where(holds, partial_rows, 0.0)
        later = (block_of > k)[:, None, None]
        solved = lax.psum(partial_rows, "blk")
        delta = jnp.einsum(
            "atw,wc->atc", strip, solved.astype(BF), preferred_element_type=F32
        )
        state = state - jnp.where(later, delta, 0.0)
        own_tile = lax.dynamic_slice_in_dim(solved, offset * span, span, 0)
        placed = lax.dynamic_update_index_in_dim(state, own_tile, local, 0)
        return jnp.where(holds, placed, state)

    def backward(k, which, state):
        holds, local, offset = locate(k)
        strip = strips[which]
        known = jnp.where((block_of > k)[:, None, None], state, 0.0).astype(BF)
        term = -jnp.einsum("atw,atc->wc", strip, known, preferred_element_type=F32)
        current = lax.dynamic_index_in_dim(state, local, 0, keepdims=False)
        placed_rows = lax.dynamic_update_slice_in_dim(
            jnp.zeros((width, columns), F32), current, offset * span, 0
        )
        term = term + jnp.where(holds, placed_rows, 0.0)
        summed = lax.psum(term, "blk").astype(BF)
        inv_tile = lax.dynamic_index_in_dim(dinv_rows, local, 0, keepdims=False)
        solved_tile = jnp.dot(inv_tile, summed, preferred_element_type=F32)
        placed = lax.dynamic_update_index_in_dim(state, solved_tile, local, 0)
        return jnp.where(holds, placed, state)

    fwd_out = forward(start, 0, fwd_state)
    fwd_out = forward(start + 1, 1, fwd_out)
    back_out = backward(start + 1, 1, back_state)
    back_out = backward(start, 0, back_out)
    return (fwd_out, back_out)


SLOT, OWNS, PANEL, PLANE, CHIP, CORE, KEEP, IS_A = range(8)


def scalars(values):
    lane = lax.broadcasted_iota(jnp.int32, (8,), 0)
    out = jnp.zeros((8,), jnp.int32)
    for i, value in enumerate(values):
        out = jnp.where(lane == i, value.astype(jnp.int32), out)
    return out


def prep_kernel(s, e_ref, w_ref, f_ref, e4_ref, w4_ref, ft_ref):
    for q in range(4):
        e4_ref[q] = e_ref[0]
        w4_ref[q] = w_ref[0, 0]
    ft_ref[...] = f_ref[0].T


def prep(s, strips, dinv_rows, fwd_state):
    tiles, span, columns = fwd_state.shape
    width = strips.shape[3]
    half = span // 2
    return pl.pallas_call(
        prep_kernel,
        grid_spec=pltpu.PrefetchScalarGridSpec(
            num_scalar_prefetch=1,
            grid=(1,),
            in_specs=[
                pl.BlockSpec((1, half, width), lambda i, s: (s[SLOT], s[CORE], 0)),
                pl.BlockSpec((1, 1, half, width), lambda i, s: (0, s[SLOT], s[CORE], 0)),
                pl.BlockSpec((1, span, columns), lambda i, s: (s[SLOT], 0, 0)),
            ],
            out_specs=[
                pl.BlockSpec((4, half, width), lambda i, s: (0, 0, 0)),
                pl.BlockSpec((4, half, width), lambda i, s: (0, 0, 0)),
                pl.BlockSpec((columns, span), lambda i, s: (0, 0)),
            ],
        ),
        out_shape=[
            jax.ShapeDtypeStruct((4, half, width), BF),
            jax.ShapeDtypeStruct((4, half, width), BF),
            jax.ShapeDtypeStruct((columns, span), F32),
        ],
        compiler_params=pltpu.CompilerParams(vmem_limit_bytes=VMEM),
        name="prep",
    )(s, dinv_rows, strips, fwd_state)


def sums_kernel(s, keep_ref, send_ref, b_ref, keep_out, send_out, copy_out, keep_acc, send_acc):
    a = pl.program_id(0)
    span = b_ref.shape[1]

    @pl.when(a == 0)
    def _():
        keep_acc[...] = jnp.zeros_like(keep_acc)
        send_acc[...] = jnp.zeros_like(send_acc)

    copy_out[...] = b_ref[...]

    @pl.when(4 * a + s[PLANE] > s[PANEL] + 1)
    def _():
        bt = b_ref[0].T.astype(BF)
        keep_acc[...] += mm(bt, keep_ref[0, 0], NN)
        send_acc[...] += mm(bt, send_ref[0, 0], NN)

    @pl.when((a == s[SLOT]) & (s[OWNS] == 1))
    def _():
        at = pl.ds(pl.multiple_of(s[CHIP] * span, span), span)
        keep_acc[:, at] = keep_acc[:, at] - b_ref[0].T

    @pl.when(a == pl.num_programs(0) - 1)
    def _():
        keep_out[...] = keep_acc[...] * SUM_SCALE
        send_out[...] = send_acc[...] * SUM_SCALE


def sums(s, strips, back_state):
    tiles, span, columns = back_state.shape
    width = strips.shape[3]
    return pl.pallas_call(
        sums_kernel,
        grid_spec=pltpu.PrefetchScalarGridSpec(
            num_scalar_prefetch=1,
            grid=(tiles,),
            in_specs=[
                pl.BlockSpec((1, 1, span, width), lambda a, s: (s[KEEP], a, 0, 0)),
                pl.BlockSpec((1, 1, span, width), lambda a, s: (1 - s[KEEP], a, 0, 0)),
                pl.BlockSpec((1, span, columns), lambda a, s: (a, 0, 0)),
            ],
            out_specs=[
                pl.BlockSpec((columns, width), lambda a, s: (0, 0)),
                pl.BlockSpec((columns, width), lambda a, s: (0, 0)),
                pl.BlockSpec((1, span, columns), lambda a, s: (a, 0, 0)),
            ],
            scratch_shapes=[
                pltpu.VMEM((columns, width), F32),
                pltpu.VMEM((columns, width), F32),
            ],
        ),
        out_shape=[
            jax.ShapeDtypeStruct((columns, width), F32),
            jax.ShapeDtypeStruct((columns, width), F32),
            jax.ShapeDtypeStruct(back_state.shape, F32),
        ],
        compiler_params=pltpu.CompilerParams(vmem_limit_bytes=VMEM),
        name="sums",
    )(s, strips, strips, back_state)


def joined(mine, other, core, full):
    half = mine.shape[1]
    for q in range(4):
        full[q, pl.ds(pl.multiple_of(core * half, half), half), :] = mine[q]
        full[q, pl.ds(pl.multiple_of((1 - core) * half, half), half), :] = other[q]


def first_kernel(s, ft, e0, e1, hi, lo, e):
    joined(e0, e1, s[CORE], e)
    x = jnp.zeros(hi.shape, F32)
    for q in range(4):
        x += mm(ft[q].astype(BF), e[q], NN)
    hi[...] = x.astype(BF)
    lo[...] = (x - x.astype(BF).astype(F32)).astype(BF)


def second_kernel(s, ft, xp, e0, e1, w0, w1, lo_a, hi, lo, e, w):
    joined(e0, e1, s[CORE], e)
    joined(w0, w1, s[CORE], w)
    x = jnp.zeros(hi.shape, F32)
    for q in range(4):
        f = ft[q] - mm(xp[...], w[q], NT)
        x += mm(f.astype(BF), e[q], NN)
    hi[...] = x.astype(BF)
    rest = (x - x.astype(BF).astype(F32)).astype(BF)
    lo[...] = jnp.where(s[IS_A] == 1, lo_a[...].astype(F32), rest.astype(F32)).astype(BF)


def third_kernel(s, tot, e0, e1, w0, w1, y, r, e, w):
    joined(e0, e1, s[CORE], e)
    joined(w0, w1, s[CORE], w)
    rest = (-tot[...]).astype(BF)
    back = jnp.zeros(r.shape, F32)
    for q in range(4):
        yq = mm(rest, e[q], NT)
        y[q] = yq
        back += mm(yq.astype(BF), w[q], NN)
    r[...] = back


def fourth_kernel(s, tot, r, e0, e1, y1, y, e):
    joined(e0, e1, s[CORE], e)
    rest = (-tot[...] - r[...]).astype(BF)
    for q in range(4):
        y[q] = jnp.where(s[IS_A] == 1, mm(rest, e[q], NT), y1[q])


def small(kernel, name, s, arrays, outs, matrices, span, width):
    vmem = pl.BlockSpec(memory_space=pltpu.VMEM)
    return pl.pallas_call(
        kernel,
        in_specs=[pl.BlockSpec(memory_space=pltpu.SMEM)] + [vmem] * len(arrays),
        out_specs=[vmem] * len(outs),
        out_shape=outs,
        scratch_shapes=[pltpu.VMEM((4, span, width), BF)] * matrices,
        compiler_params=pltpu.CompilerParams(vmem_limit_bytes=VMEM),
        name=name,
    )(s, *arrays)


def update_kernel(s, f_ref, w0_ref, w1_ref, xp_ref, xq_ref, lo_ref, out_ref):
    a = pl.program_id(0)
    span = f_ref.shape[1]
    quarter = lo_ref.shape[1]
    block = 4 * a + s[PLANE]
    own = (a == s[SLOT]) & (s[OWNS] == 1)

    @pl.when(own & (s[IS_A] == 1))
    def _():
        at = pl.ds(pl.multiple_of(s[CHIP] * span, span), span)
        for q in range(4):
            x = xp_ref[q, :, at].astype(F32) + lo_ref[q].astype(F32)
            out_ref[0, :, q * quarter:(q + 1) * quarter] = x.T

    @pl.when(own & (s[IS_A] == 0))
    def _():
        at = pl.ds(pl.multiple_of(s[CHIP] * span, span), span)
        for q in range(4):
            x = xq_ref[q, :, at].astype(F32) + lo_ref[q].astype(F32)
            out_ref[0, :, q * quarter:(q + 1) * quarter] = x.T

    @pl.when(block > s[PANEL] + 1)
    def _():
        for q in range(4):
            at = slice(q * quarter, (q + 1) * quarter)
            d0 = mm(w0_ref[0, 0], xp_ref[q], NT)
            d1 = mm(w1_ref[0, 0], xq_ref[q], NT)
            out_ref[0, :, at] = (f_ref[0, :, at] - d0) - d1

    @pl.when(block < s[PANEL])
    def _():
        out_ref[...] = f_ref[...]


def update(s, fwd_state, strips, xp, xq, lo):
    tiles, span, columns = fwd_state.shape
    width = strips.shape[3]
    quarter = columns // 4
    return pl.pallas_call(
        update_kernel,
        grid_spec=pltpu.PrefetchScalarGridSpec(
            num_scalar_prefetch=1,
            grid=(tiles,),
            in_specs=[
                pl.BlockSpec((1, span, columns), lambda a, s: (a, 0, 0)),
                pl.BlockSpec((1, 1, span, width), lambda a, s: (0, a, 0, 0)),
                pl.BlockSpec((1, 1, span, width), lambda a, s: (1, a, 0, 0)),
                pl.BlockSpec((4, quarter, width), lambda a, s: (0, 0, 0)),
                pl.BlockSpec((4, quarter, width), lambda a, s: (0, 0, 0)),
                pl.BlockSpec((4, quarter, span), lambda a, s: (0, 0, 0)),
            ],
            out_specs=pl.BlockSpec((1, span, columns), lambda a, s: (a, 0, 0)),
        ),
        out_shape=jax.ShapeDtypeStruct(fwd_state.shape, F32),
        compiler_params=pltpu.CompilerParams(vmem_limit_bytes=VMEM),
        name="update",
    )(s, fwd_state, strips, strips, xp, xq, lo)


def place_kernel(s, copy_ref, y_ref, out_ref):
    quarter = y_ref.shape[1]

    @pl.when(s[OWNS] == 1)
    def _():
        for q in range(4):
            out_ref[0, :, q * quarter:(q + 1) * quarter] = y_ref[q].T

    @pl.when(s[OWNS] == 0)
    def _():
        out_ref[...] = copy_ref[...]


def place(s, copy, y):
    tiles, span, columns = copy.shape
    tile = pl.BlockSpec((1, span, columns), lambda i, s: (s[SLOT], 0, 0))
    return pl.pallas_call(
        place_kernel,
        grid_spec=pltpu.PrefetchScalarGridSpec(
            num_scalar_prefetch=1,
            grid=(1,),
            in_specs=[tile, pl.BlockSpec(y.shape, lambda i, s: (0, 0, 0))],
            out_specs=tile,
        ),
        out_shape=jax.ShapeDtypeStruct(copy.shape, F32),
        input_output_aliases={1: 0},
        compiler_params=pltpu.CompilerParams(vmem_limit_bytes=VMEM),
        name="place",
    )(s, copy, y)


def plane_body(panel, strips, dinv_rows, fwd_state, back_state):
    tiles, span, columns = fwd_state.shape
    width = strips.shape[3]
    half, quarter = span // 2, columns // 4
    device = lax.axis_index("blk")
    plane, chip, core = device // 4, device % 4, lax.axis_index("rhs")
    start = panel[0]
    groups = [[4 * z + j for j in range(4)] for z in range(4)]

    def exchange(x):
        return lax.all_to_all(x, "blk", 0, 0, axis_index_groups=groups, tiled=True)

    def hop(x, *pairs):
        return lax.ppermute(
            x, "blk", [(4 * a + j, 4 * b + j) for a, b in pairs for j in range(4)]
        )

    def swap(x):
        return lax.ppermute(x, "rhs", [(0, 1), (1, 0)])

    def branch(first):
        A, B = first, (first + 1) % 4
        others = [z for z in range(4) if z not in (A, B)]
        if A // 2 == B // 2:
            near = others[0] if abs(others[0] - B) <= abs(others[1] - B) else others[1]
            keeps = [B, near]
        else:
            keeps = [B, A ^ 1]
        ones = [z for z in keeps if z != B][0]
        zeros = [z for z in others if z != ones][0]

        def run(panel, strips, dinv_rows, fwd_state, back_state):
            is_a, is_b = plane == A, plane == B
            slot = start // 4 + (jnp.where(is_b, 1, 0) if first == 3 else 0)
            keep = functools.reduce(jnp.logical_or, [plane == z for z in keeps])
            s = scalars([slot, is_a | is_b, start, plane, chip, core, keep, is_a])

            e4, w4, ft = prep(s, strips, dinv_rows, fwd_state)
            ft = exchange(ft).reshape(4, quarter, span)
            e0 = exchange(e4.reshape(4 * half, width)).reshape(4, half, width)
            w0 = exchange(w4.reshape(4 * half, width)).reshape(4, half, width)
            e1, w1 = swap(e0), swap(w0)

            kept, sent, copy = sums(s, strips, back_state)
            got = lax.ppermute(sent.astype(HF), "blk", [(i, i ^ 4) for i in range(16)])
            pair = (kept + got.astype(F32)).astype(HF)
            parts = exchange(pair).reshape(4, quarter, width)
            part = jnp.sum(parts.astype(F32), axis=0)
            far = hop(part.astype(HF), (ones, B), (zeros, A))
            tot = (part + far.astype(F32)) * (1.0 / SUM_SCALE)

            piece = jax.ShapeDtypeStruct((quarter, width), BF)
            piece32 = jax.ShapeDtypeStruct((quarter, width), F32)
            blocks = jax.ShapeDtypeStruct((4, quarter, span), F32)

            hi_p, lo_p = small(first_kernel, "first", s, [ft, e0, e1], [piece, piece], 1, span, width)
            hi_p = jnp.where(is_a, hi_p, jnp.zeros_like(hi_p))
            xp = hi_p + hop(hi_p, (A, B))
            if first in (1, 3):
                c, d = (A - 1, B + 1)
                xp_all = xp + hop(xp, (A, c), (B, d))
            elif first == 0:
                xp_all = xp + hop(xp, (B, 2)) + hop(xp, (B, 3))
            else:
                xp_all = xp + hop(xp, (A, 1)) + hop(xp, (A, 0))
            hi_q, lo = small(
                second_kernel, "second", s, [ft, xp, e0, e1, w0, w1, lo_p], [piece, piece], 2, span, width
            )
            hi_q = jnp.where(is_b, hi_q, jnp.zeros_like(hi_q))
            xq_all = hi_q
            for z in range(4):
                if z != B:
                    xq_all = xq_all + hop(hi_q, (B, z))

            def gather(x):
                four = jnp.broadcast_to(x[None], (4,) + x.shape)
                return exchange(four.reshape(columns, width)).reshape(4, quarter, width)

            xp_full, xq_full = gather(xp_all), gather(xq_all)
            lo4 = lo.reshape(quarter, 4, span).transpose(1, 0, 2).reshape(columns, span)
            lo_own = exchange(lo4).reshape(4, quarter, span)
            fwd_out = update(s, fwd_state, strips, xp_full, xq_full, lo_own)

            y1, r = small(third_kernel, "third", s, [tot, e0, e1, w0, w1], [blocks, piece32], 2, span, width)
            r = hop(r, (B, A))
            (y,) = small(fourth_kernel, "fourth", s, [tot, r, e0, e1, y1], [blocks], 1, span, width)
            y_own = exchange(y.reshape(columns, span)).reshape(4, quarter, span)
            back_out = place(s, copy, y_own)
            return fwd_out, back_out

        return run

    return lax.switch(
        jnp.mod(start, 4),
        [branch(z) for z in range(4)],
        panel, strips, dinv_rows, fwd_state, back_state,
    )


def body(panel, strips, dinv_rows, fwd_state, back_state):
    tiles, span, columns = fwd_state.shape
    width = strips.shape[3]
    blocks = lax.axis_size("blk")
    regular = (
        blocks == 16
        and lax.axis_size("rhs") == 2
        and width == 4 * span
        and span % 256 == 0
        and columns % 512 == 0
    )
    chosen = plane_body if regular else plain_body
    return chosen(panel, strips, dinv_rows, fwd_state, back_state)


def solution(mesh):
    return jax.shard_map(
        body,
        mesh=mesh,
        in_specs=(
            P(),
            P(None, None, "blk", None),
            P(None, "blk", None),
            P(None, "blk", "rhs"),
            P(None, "blk", "rhs"),
        ),
        out_specs=(P(None, "blk", "rhs"), P(None, "blk", "rhs")),
        check_vma=False,
    )
```

```python
import jax
import jax.numpy as jnp
from jax import lax
from jax.experimental import pallas as pl
from jax.experimental.pallas import tpu as pltpu
from jax.sharding import PartitionSpec as P

BF = jnp.bfloat16
HF = jnp.float16
F32 = jnp.float32
SUM_SCALE = 4.0
VMEM = 100 * 1024 * 1024 // 2

NT = (((1,), (1,)), ((), ()))
NN = (((1,), (0,)), ((), ()))


def mm(a, b, dims):
    return lax.dot_general(a, b, dims, preferred_element_type=F32)


def plain_body(panel, strips, dinv_rows, fwd_state, back_state):
    tiles, span, columns = fwd_state.shape
    width = strips.shape[3]
    per_panel = width // span
    blocks = lax.axis_size("blk")
    device = lax.axis_index("blk")
    start = panel[0]
    slots = jnp.arange(tiles, dtype=jnp.int32)
    block_of = (slots * blocks + device) // per_panel

    def locate(k):
        offset = jnp.mod(device - per_panel * k, blocks)
        holds = offset < per_panel
        local = jnp.clip((per_panel * k + offset) // blocks, 0, tiles - 1)
        return (holds, local, jnp.minimum(offset, per_panel - 1))

    def forward(k, which, state):
        holds, local, offset = locate(k)
        strip = strips[which]
        current = lax.dynamic_index_in_dim(state, local, 0, keepdims=False).astype(BF)
        inv_tile = lax.dynamic_index_in_dim(dinv_rows, local, 0, keepdims=False)
        partial_rows = lax.dot_general(
            inv_tile, current, (((0,), (0,)), ((), ())), preferred_element_type=F32
        )
        partial_rows = jnp.where(holds, partial_rows, 0.0)
        later = (block_of > k)[:, None, None]
        solved = lax.psum(partial_rows, "blk")
        delta = jnp.einsum(
            "atw,wc->atc", strip, solved.astype(BF), preferred_element_type=F32
        )
        state = state - jnp.where(later, delta, 0.0)
        own_tile = lax.dynamic_slice_in_dim(solved, offset * span, span, 0)
        placed = lax.dynamic_update_index_in_dim(state, own_tile, local, 0)
        return jnp.where(holds, placed, state)

    def backward(k, which, state):
        holds, local, offset = locate(k)
        strip = strips[which]
        known = jnp.where((block_of > k)[:, None, None], state, 0.0).astype(BF)
        term = -jnp.einsum("atw,atc->wc", strip, known, preferred_element_type=F32)
        current = lax.dynamic_index_in_dim(state, local, 0, keepdims=False)
        placed_rows = lax.dynamic_update_slice_in_dim(
            jnp.zeros((width, columns), F32), current, offset * span, 0
        )
        term = term + jnp.where(holds, placed_rows, 0.0)
        summed = lax.psum(term, "blk").astype(BF)
        inv_tile = lax.dynamic_index_in_dim(dinv_rows, local, 0, keepdims=False)
        solved_tile = jnp.dot(inv_tile, summed, preferred_element_type=F32)
        placed = lax.dynamic_update_index_in_dim(state, solved_tile, local, 0)
        return jnp.where(holds, placed, state)

    fwd_out = forward(start, 0, fwd_state)
    fwd_out = forward(start + 1, 1, fwd_out)
    back_out = backward(start + 1, 1, back_state)
    back_out = backward(start, 0, back_out)
    return (fwd_out, back_out)


SLOT, OWNS, PANEL, PLANE, CHIP, CORE, KEEP, IS_A, FIRST, LOW = range(10)


def scalars(values):
    lane = lax.broadcasted_iota(jnp.int32, (16,), 0)
    out = jnp.zeros((16,), jnp.int32)
    for i, value in enumerate(values):
        out = jnp.where(lane == i, value.astype(jnp.int32), out)
    return out


def call(kernel, name, s, grid, ins, outs, shapes, arrays, scratch=(), aliases=None):
    return pl.pallas_call(
        kernel,
        grid_spec=pltpu.PrefetchScalarGridSpec(
            num_scalar_prefetch=1, grid=grid, in_specs=ins, out_specs=outs, scratch_shapes=list(scratch)
        ),
        out_shape=shapes,
        input_output_aliases=aliases or {},
        compiler_params=pltpu.CompilerParams(vmem_limit_bytes=VMEM),
        name=name,
    )(s, *arrays)


def whole(*shape):
    return pl.BlockSpec(shape, lambda i, s: (0,) * len(shape))


def shaped(dtype, *shape):
    return jax.ShapeDtypeStruct(shape, dtype)


def prep_kernel(s, e_ref, w_ref, f_ref, eh_ref, wh_ref, fq_ref):
    quarter = fq_ref.shape[2]
    eh_ref[...] = e_ref[0]
    wh_ref[...] = w_ref[0, 0]
    for q in range(4):
        fq_ref[q] = f_ref[0, :, q * quarter:(q + 1) * quarter]


def prep(s, strips, dinv_rows, fwd_state):
    tiles, span, columns = fwd_state.shape
    width = strips.shape[3]
    half, quarter = span // 2, columns // 4
    return call(
        prep_kernel, "prep", s, (1,),
        [
            pl.BlockSpec((1, half, width), lambda i, s: (s[SLOT], s[CORE], 0)),
            pl.BlockSpec((1, 1, half, width), lambda i, s: (0, s[SLOT], s[CORE], 0)),
            pl.BlockSpec((1, span, columns), lambda i, s: (s[SLOT], 0, 0)),
        ],
        [whole(half, width), whole(half, width), whole(4, span, quarter)],
        [shaped(BF, half, width), shaped(BF, half, width), shaped(F32, 4, span, quarter)],
        (dinv_rows, strips, fwd_state),
    )


def send_kernel(s, w_ref, b_ref, out_ref):
    a = pl.program_id(0)

    @pl.when(a == 0)
    def _():
        out_ref[...] = jnp.zeros_like(out_ref)

    @pl.when(4 * a + s[PLANE] > s[PANEL] + 1)
    def _():
        out_ref[...] += mm((b_ref[0] * SUM_SCALE).T.astype(BF), w_ref[0, 0], NN)


def keep_kernel(s, w_ref, b_ref, out_ref, copy_ref):
    a = pl.program_id(0)
    span = b_ref.shape[1]
    copy_ref[...] = b_ref[...]
    send_kernel(s, w_ref, b_ref, out_ref)

    @pl.when((a == s[SLOT]) & (s[OWNS] == 1))
    def _():
        at = pl.ds(pl.multiple_of(s[CHIP] * span, span), span)
        out_ref[:, at] = out_ref[:, at] - (b_ref[0] * SUM_SCALE).T


def sums_send(s, strips, back_state):
    tiles, span, columns = back_state.shape
    width = strips.shape[3]
    return call(
        send_kernel, "sums_send", s, (tiles,),
        [
            pl.BlockSpec((1, 1, span, width), lambda a, s: (1 - s[KEEP], jnp.maximum(a, s[FIRST]), 0, 0)),
            pl.BlockSpec((1, span, columns), lambda a, s: (jnp.maximum(a, s[FIRST]), 0, 0)),
        ],
        whole(columns, width),
        shaped(F32, columns, width),
        (strips, back_state),
    )


def sums_keep(s, strips, back_state):
    tiles, span, columns = back_state.shape
    width = strips.shape[3]
    tile = pl.BlockSpec((1, span, columns), lambda a, s: (a, 0, 0))
    return call(
        keep_kernel, "sums_keep", s, (tiles,),
        [
            pl.BlockSpec((1, 1, span, width), lambda a, s: (s[KEEP], jnp.maximum(a, s[FIRST]), 0, 0)),
            tile,
        ],
        [whole(columns, width), tile],
        [shaped(F32, columns, width), shaped(F32, *back_state.shape)],
        (strips, back_state),
    )


def join(full, d, mine, other, core):
    half = mine.shape[0]
    full[d, pl.ds(pl.multiple_of(core * half, half), half), :] = mine[...]
    full[d, pl.ds(pl.multiple_of((1 - core) * half, half), half), :] = other[...]


def split(x):
    high = x.astype(BF)
    return high, (x - high.astype(F32)).astype(BF)


def first_kernel(s, fq, own, m1, m2, m3, o1, o2, o3, hi, lo, e):
    span = fq.shape[1]
    e[0] = own[0]
    for d, mine, other in ((1, m1, o1), (2, m2, o2), (3, m3, o3)):
        join(e, d, mine, other, s[CORE])
    x = jnp.zeros(hi.shape, F32)
    for d in range(4):
        x += mm(fq[s[CHIP] ^ d].T.astype(BF), e[d], NN)
    high, low = split(x)
    hi[...] = high
    for q in range(4):
        lo[q] = low[:, q * span:(q + 1) * span]


def second_kernel(s, fq, xp, e, m0, m1, m2, m3, o0, o1, o2, o3, lo_a, hi, lo, w):
    span = fq.shape[1]
    for d, mine, other in ((0, m0, o0), (1, m1, o1), (2, m2, o2), (3, m3, o3)):
        join(w, d, mine, other, s[CORE])
    x = jnp.zeros(hi.shape, F32)
    for d in range(4):
        f = fq[s[CHIP] ^ d].T - mm(xp[...], w[d], NT)
        x += mm(f.astype(BF), e[d], NN)
    high, low = split(x)
    hi[...] = high

    @pl.when(s[IS_A] == 1)
    def _():
        lo[...] = lo_a[...]

    @pl.when(s[IS_A] == 0)
    def _():
        for q in range(4):
            lo[q] = low[:, q * span:(q + 1) * span]


def third_kernel(s, part, far, e, y, high):
    span = y.shape[2]
    rest = ((part[...] + far[...]) * (-1.0 / SUM_SCALE)).astype(BF)
    for d in range(4):
        q = s[CHIP] ^ d
        yq = mm(rest, e[d], NT)
        y[q] = yq
        high[:, pl.ds(pl.multiple_of(q * span, span), span)] = yq.astype(BF)


def fourth_kernel(s, part, far, high, e, w, y_b, y):
    span = y.shape[2]

    @pl.when(s[IS_A] == 0)
    def _():
        y[...] = y_b[...]

    @pl.when(s[IS_A] == 1)
    def _():
        rest = (part[...] + far[...]) * (-1.0 / SUM_SCALE)
        for d in range(4):
            at = pl.ds(pl.multiple_of((s[CHIP] ^ d) * span, span), span)
            rest -= mm(high[:, at], w[d], NN)
        rest = rest.astype(BF)
        for d in range(4):
            y[s[CHIP] ^ d] = mm(rest, e[d], NT)


def fill(x_full, pieces, chip):
    for d, piece in enumerate(pieces):
        x_full[chip ^ d] = piece[...]


def update_one_kernel(s, f_ref, w_ref, x0, x1, x2, x3, out_ref, x_full):
    a = pl.program_id(0)

    @pl.when(a == 0)
    def _():
        fill(x_full, (x0, x1, x2, x3), s[CHIP])

    later = 4 * a + s[PLANE] > s[PANEL] + 1

    @pl.when(later)
    def _():
        x = x_full[...].reshape(-1, x_full.shape[2])
        out_ref[0] = f_ref[0] - mm(w_ref[0, 0], x, NT)

    @pl.when(jnp.logical_not(later))
    def _():
        out_ref[...] = f_ref[...]


def update_two_kernel(s, f_ref, w_ref, x0, x1, x2, x3, p0, p1, p2, p3, lo_ref, out_ref, x_full):
    a = pl.program_id(0)
    span = f_ref.shape[1]
    quarter = lo_ref.shape[1]
    own = (a == s[SLOT]) & (s[OWNS] == 1)

    @pl.when(a == 0)
    def _():
        fill(x_full, (x0, x1, x2, x3), s[CHIP])

    @pl.when(4 * a + s[PLANE] > s[PANEL] + 1)
    def _():
        x = x_full[...].reshape(-1, x_full.shape[2])
        out_ref[0] = f_ref[0] - mm(w_ref[0, 0], x, NT)

    def solved(pieces):
        at = pl.ds(pl.multiple_of(s[CHIP] * span, span), span)
        for d, piece in enumerate(pieces):
            q = s[CHIP] ^ d
            x = piece[:, at].astype(F32) + lo_ref[q].astype(F32)
            out_ref[0, :, pl.ds(pl.multiple_of(q * quarter, quarter), quarter)] = x.T

    @pl.when(own & (s[IS_A] == 1))
    def _():
        solved((p0, p1, p2, p3))

    @pl.when(own & (s[IS_A] == 0))
    def _():
        solved((x0, x1, x2, x3))

    @pl.when((a == s[LOW]) & (4 * a + s[PLANE] <= s[PANEL] + 1) & jnp.logical_not(own))
    def _():
        out_ref[...] = f_ref[...]


def update_one(s, fwd_state, strips, pieces):
    tiles, span, columns = fwd_state.shape
    width = strips.shape[3]
    tile = pl.BlockSpec((1, span, columns), lambda a, s: (a, 0, 0))
    return call(
        update_one_kernel, "update_one", s, (tiles,),
        [tile, pl.BlockSpec((1, 1, span, width), lambda a, s: (0, jnp.maximum(a, s[FIRST]), 0, 0))]
        + [whole(columns // 4, width)] * 4,
        tile, shaped(F32, *fwd_state.shape),
        (fwd_state, strips, *pieces),
        scratch=[pltpu.VMEM((4, columns // 4, width), BF)],
    )


def update_two(s, state, strips, pieces, pieces_p, lo):
    tiles, span, columns = state.shape
    width = strips.shape[3]
    tile = pl.BlockSpec((1, span, columns), lambda a, s: (jnp.maximum(a, s[LOW]), 0, 0))
    return call(
        update_two_kernel, "update_two", s, (tiles,),
        [tile, pl.BlockSpec((1, 1, span, width), lambda a, s: (1, jnp.maximum(a, s[FIRST]), 0, 0))]
        + [whole(columns // 4, width)] * 8 + [whole(*lo.shape)],
        tile, shaped(F32, *state.shape),
        (state, strips, *pieces, *pieces_p, lo),
        scratch=[pltpu.VMEM((4, columns // 4, width), BF)],
        aliases={1: 0},
    )


def place_kernel(s, copy_ref, y_ref, out_ref):
    quarter = y_ref.shape[1]

    @pl.when(s[OWNS] == 1)
    def _():
        for q in range(4):
            out_ref[0, :, q * quarter:(q + 1) * quarter] = y_ref[q].T

    @pl.when(s[OWNS] == 0)
    def _():
        out_ref[...] = copy_ref[...]


def place(s, copy, y):
    tiles, span, columns = copy.shape
    tile = pl.BlockSpec((1, span, columns), lambda i, s: (s[SLOT], 0, 0))
    return call(
        place_kernel, "place", s, (1,), [tile, whole(*y.shape)], tile,
        shaped(F32, *copy.shape), (copy, y), aliases={1: 0},
    )


def after(x, *waits):
    return lax.optimization_barrier((x,) + waits)[0]


def plane_body(panel, strips, dinv_rows, fwd_state, back_state):
    tiles, span, columns = fwd_state.shape
    width = strips.shape[3]
    half, quarter = span // 2, columns // 4
    device = lax.axis_index("blk")
    plane, chip, core = device // 4, device % 4, lax.axis_index("rhs")
    start = panel[0]
    home = lax.rem(start, 4)
    is_a = plane == home
    is_b = plane == lax.rem(start + 1, 4)
    groups = [[4 * z + j for j in range(4)] for z in range(4)]

    def exchange(x):
        return lax.all_to_all(x, "blk", 0, 0, axis_index_groups=groups, tiled=True)

    def permute(x, to):
        return lax.ppermute(x, "blk", [(i, to(i)) for i in range(16)])

    def up(x):
        return permute(x, lambda i: (i + 4) % 16)

    def down(x):
        return permute(x, lambda i: (i + 12) % 16)

    def across(x):
        return permute(x, lambda i: i ^ 8)

    def gather(x):
        return [permute(x, lambda i, d=d: i ^ d) for d in (1, 2, 3)]

    def swap(x):
        return lax.ppermute(x, "rhs", [(0, 1), (1, 0)])

    slot = start // 4 + jnp.where(is_b & (home == 3), 1, 0)
    keep = lax.rem(plane + start + 1, 2) == 0
    first_later = jnp.clip((start + 5 - plane) // 4, 0, tiles - 1)
    low = jnp.minimum(first_later, jnp.where(is_a | is_b, slot, tiles - 1))
    s = scalars([slot, is_a | is_b, start, plane, chip, core, keep, is_a, first_later, low])

    sent = sums_send(s, strips, back_state).astype(HF)
    got = permute(sent, lambda i: i ^ 4)

    eh, wh, fq = prep(s, strips, dinv_rows, fwd_state)
    e_mine = gather(eh)
    fq = exchange(fq.reshape(4 * span, quarter)).reshape(4, span, quarter)
    wh = jnp.where(is_a, down(wh), wh)
    e_other = [swap(x) for x in e_mine]

    piece = shaped(BF, quarter, width)
    lows = shaped(BF, 4, quarter, span)
    matrix = shaped(BF, 4, span, width)
    thin, thick = whole(half, width), whole(quarter, width)

    hi_p, lo_p, e = call(
        first_kernel, "first", s, (1,),
        [whole(4, span, quarter), pl.BlockSpec((1, span, width), lambda i, s: (s[SLOT], 0, 0))] + [thin] * 6,
        [thick, whole(4, quarter, span), whole(4, span, width)], [piece, lows, matrix],
        (fq, dinv_rows, *e_mine, *e_other),
    )
    below = up(hi_p)
    w_mine = [wh] + gather(wh)
    w_other = [swap(x) for x in w_mine]
    kept, copy = sums_keep(s, strips, back_state)

    xp = jnp.where(is_a, hi_p, below)
    xp_far = across(xp)
    hi_q, lo, w = call(
        second_kernel, "second", s, (1,),
        [whole(4, span, quarter), thick, whole(4, span, width)] + [thin] * 8 + [whole(4, quarter, span)],
        [thick, whole(4, quarter, span), whole(4, span, width)], [piece, lows, matrix],
        (fq, xp, e, *w_mine, *w_other, lo_p),
    )

    def spread(first):
        source = (first + 1) % 4

        def run(x):
            total = x
            for z in range(4):
                if z != source:
                    total = total + lax.ppermute(
                        x, "blk", [(4 * source + j, 4 * z + j) for j in range(4)]
                    )
            return total

        return run

    hi_q = jnp.where(is_b, hi_q, jnp.zeros_like(hi_q))
    xq = lax.switch(home, [spread(z) for z in range(4)], hi_q)
    lo_own = exchange(lo.reshape(columns, span)).reshape(4, quarter, span)
    xp = jnp.where(is_a | is_b, xp, xp_far)
    xp_all = [xp] + gather(xp)
    state = update_one(s, fwd_state, strips, xp_all)
    xq_all = [xq] + gather(xq)
    fwd_out = update_two(s, state, strips, xq_all, xp_all, lo_own)

    pair = (kept + got.astype(F32)).astype(HF)
    parts = exchange(pair).reshape(4, quarter, width)
    part = jnp.sum(parts.astype(F32), axis=0)
    far = across(part.astype(HF)).astype(F32)
    y_b, high = call(
        third_kernel, "third", s, (1,), [thick, thick, whole(4, span, width)],
        [whole(4, quarter, span), thick], [shaped(F32, 4, quarter, span), piece],
        (part, far, e),
    )
    high = down(high)
    y = call(
        fourth_kernel, "fourth", s, (1,),
        [thick, thick, thick, whole(4, span, width), whole(4, span, width), whole(4, quarter, span)],
        whole(4, quarter, span), shaped(F32, 4, quarter, span),
        (part, far, high, e, w, y_b),
    )
    y_own = exchange(y.reshape(columns, span)).reshape(4, quarter, span)
    back_out = place(s, copy, y_own)
    return fwd_out, back_out


def body(panel, strips, dinv_rows, fwd_state, back_state):
    tiles, span, columns = fwd_state.shape
    width = strips.shape[3]
    blocks = lax.axis_size("blk")
    regular = (
        blocks == 16
        and lax.axis_size("rhs") == 2
        and width == 4 * span
        and span % 256 == 0
        and columns % 512 == 0
    )
    chosen = plane_body if regular else plain_body
    return chosen(panel, strips, dinv_rows, fwd_state, back_state)


def solution(mesh):
    return jax.shard_map(
        body,
        mesh=mesh,
        in_specs=(
            P(),
            P(None, None, "blk", None),
            P(None, "blk", None),
            P(None, "blk", "rhs"),
            P(None, "blk", "rhs"),
        ),
        out_specs=(P(None, "blk", "rhs"), P(None, "blk", "rhs")),
        check_vma=False,
    )
```

```python
import jax
import jax.numpy as jnp
from jax import lax
from jax.experimental import pallas as pl
from jax.experimental.pallas import tpu as pltpu
from jax.sharding import PartitionSpec as P

BF = jnp.bfloat16
HF = jnp.float16
F32 = jnp.float32
SUM_SCALE = 4.0
MIB = 1024 * 1024

NN = (((1,), (0,)), ((), ()))


def mm(a, b, dims):
    return lax.dot_general(a, b, dims, preferred_element_type=F32)


def plain_body(panel, strips, dinv_rows, fwd_state, back_state):
    tiles, span, columns = fwd_state.shape
    width = strips.shape[3]
    per_panel = width // span
    blocks = lax.axis_size("blk")
    device = lax.axis_index("blk")
    start = panel[0]
    slots = jnp.arange(tiles, dtype=jnp.int32)
    block_of = (slots * blocks + device) // per_panel

    def locate(k):
        offset = jnp.mod(device - per_panel * k, blocks)
        holds = offset < per_panel
        local = jnp.clip((per_panel * k + offset) // blocks, 0, tiles - 1)
        return (holds, local, jnp.minimum(offset, per_panel - 1))

    def forward(k, which, state):
        holds, local, offset = locate(k)
        strip = strips[which]
        current = lax.dynamic_index_in_dim(state, local, 0, keepdims=False).astype(BF)
        inv_tile = lax.dynamic_index_in_dim(dinv_rows, local, 0, keepdims=False)
        partial_rows = lax.dot_general(
            inv_tile, current, (((0,), (0,)), ((), ())), preferred_element_type=F32
        )
        partial_rows = jnp.where(holds, partial_rows, 0.0)
        later = (block_of > k)[:, None, None]
        solved = lax.psum(partial_rows, "blk")
        delta = jnp.einsum(
            "atw,wc->atc", strip, solved.astype(BF), preferred_element_type=F32
        )
        state = state - jnp.where(later, delta, 0.0)
        own_tile = lax.dynamic_slice_in_dim(solved, offset * span, span, 0)
        placed = lax.dynamic_update_index_in_dim(state, own_tile, local, 0)
        return jnp.where(holds, placed, state)

    def backward(k, which, state):
        holds, local, offset = locate(k)
        strip = strips[which]
        known = jnp.where((block_of > k)[:, None, None], state, 0.0).astype(BF)
        term = -jnp.einsum("atw,atc->wc", strip, known, preferred_element_type=F32)
        current = lax.dynamic_index_in_dim(state, local, 0, keepdims=False)
        placed_rows = lax.dynamic_update_slice_in_dim(
            jnp.zeros((width, columns), F32), current, offset * span, 0
        )
        term = term + jnp.where(holds, placed_rows, 0.0)
        summed = lax.psum(term, "blk").astype(BF)
        inv_tile = lax.dynamic_index_in_dim(dinv_rows, local, 0, keepdims=False)
        solved_tile = jnp.dot(inv_tile, summed, preferred_element_type=F32)
        placed = lax.dynamic_update_index_in_dim(state, solved_tile, local, 0)
        return jnp.where(holds, placed, state)

    fwd_out = forward(start, 0, fwd_state)
    fwd_out = forward(start + 1, 1, fwd_out)
    back_out = backward(start + 1, 1, back_state)
    back_out = backward(start, 0, back_out)
    return (fwd_out, back_out)


SLOT, OWNS, PANEL, PLANE, CHIP, CORE, KEEP, IS_A, FIRST, LOW = range(10)


def scalars(values):
    lane = lax.broadcasted_iota(jnp.int32, (16,), 0)
    out = jnp.zeros((16,), jnp.int32)
    for i, value in enumerate(values):
        out = jnp.where(lane == i, value.astype(jnp.int32), out)
    return out


def call(kernel, name, s, grid, ins, outs, shapes, arrays, scratch=(), aliases=None, limit=63):
    return pl.pallas_call(
        kernel,
        grid_spec=pltpu.PrefetchScalarGridSpec(
            num_scalar_prefetch=1, grid=grid, in_specs=ins, out_specs=outs, scratch_shapes=list(scratch)
        ),
        out_shape=shapes,
        input_output_aliases=aliases or {},
        compiler_params=pltpu.CompilerParams(vmem_limit_bytes=limit * MIB),
        name=name,
    )(s, *arrays)


def whole(*shape):
    return pl.BlockSpec(shape, lambda i, s: (0,) * len(shape), pipeline_mode=pl.Buffered(1))


def shaped(dtype, *shape):
    return jax.ShapeDtypeStruct(shape, dtype)


def prep_kernel(s, e_ref, w_ref, f_ref, *outs):
    half, width = e_ref.shape[1:]
    quarter = (outs[0].shape[1] - width) // 2
    for d in (1, 2, 3):
        at = pl.ds(pl.multiple_of((s[CHIP] ^ d) * quarter, quarter), quarter)
        high, low = split(f_ref[0, :, at])
        for out, matrix, f in ((outs[d - 1], e_ref[0], high), (outs[d + 2], w_ref[0, 0], low)):
            out[:, :width] = matrix
            out[:, width:width + quarter] = f[:half]
            out[:, width + quarter:] = f[half:]


def prep(s, strips, dinv_rows, fwd_state):
    tiles, span, columns = fwd_state.shape
    width = strips.shape[3]
    half, quarter = span // 2, columns // 4
    outs = call(
        prep_kernel, "prep", s, (1,),
        [
            pl.BlockSpec((1, half, width), lambda i, s: (s[SLOT], s[CORE], 0)),
            pl.BlockSpec((1, 1, half, width), lambda i, s: (0, s[SLOT], s[CORE], 0)),
            pl.BlockSpec((1, span, columns), lambda i, s: (s[SLOT], 0, 0)),
        ],
        [whole(half, width + 2 * quarter)] * 6,
        [shaped(BF, half, width + 2 * quarter)] * 6,
        (dinv_rows, strips, fwd_state),
    )
    return outs[:3], outs[3:]


def send_kernel(s, w_ref, b_ref, out_ref):
    a = pl.program_id(0)

    @pl.when(a == 0)
    def _():
        out_ref[...] = jnp.zeros_like(out_ref)

    @pl.when(4 * a + s[PLANE] > s[PANEL] + 1)
    def _():
        out_ref[...] += mm((b_ref[0] * SUM_SCALE).T.astype(BF), w_ref[0, 0], NN)


def keep_kernel(s, w_ref, b_ref, out_ref, copy_ref):
    a = pl.program_id(0)
    span = b_ref.shape[1]
    copy_ref[...] = b_ref[...]
    send_kernel(s, w_ref, b_ref, out_ref)

    @pl.when((a == s[SLOT]) & (s[OWNS] == 1))
    def _():
        at = pl.ds(pl.multiple_of(s[CHIP] * span, span), span)
        out_ref[:, at] = out_ref[:, at] - (b_ref[0] * SUM_SCALE).T


def sums_send(s, strips, back_state):
    tiles, span, columns = back_state.shape
    width = strips.shape[3]
    return call(
        send_kernel, "sums_send", s, (tiles,),
        [
            pl.BlockSpec((1, 1, span, width), lambda a, s: (1 - s[KEEP], jnp.maximum(a, s[FIRST]), 0, 0)),
            pl.BlockSpec((1, span, columns), lambda a, s: (jnp.maximum(a, s[FIRST]), 0, 0)),
        ],
        whole(columns, width),
        shaped(F32, columns, width),
        (strips, back_state),
    )


def sums_keep(s, strips, back_state):
    tiles, span, columns = back_state.shape
    width = strips.shape[3]
    tile = pl.BlockSpec((1, span, columns), lambda a, s: (a, 0, 0))
    return call(
        keep_kernel, "sums_keep", s, (tiles,),
        [
            pl.BlockSpec((1, 1, span, width), lambda a, s: (s[KEEP], jnp.maximum(a, s[FIRST]), 0, 0)),
            tile,
        ],
        [whole(columns, width), tile],
        [shaped(F32, columns, width), shaped(F32, *back_state.shape)],
        (strips, back_state),
    )


HBM = pl.BlockSpec(memory_space=pltpu.HBM)


def fetch(sems, pairs):
    copies = [pltpu.make_async_copy(a, b, sems.at[i]) for i, (a, b) in enumerate(pairs)]
    for copy in copies:
        copy.start()
    for copy in copies:
        copy.wait()


def halves(full, d, mine, other, core):
    half, width = mine.shape[0], full.shape[2]
    return [
        (mine.at[:, :width], full.at[d, pl.ds(pl.multiple_of(core * half, half), half), :]),
        (other.at[:, :width], full.at[d, pl.ds(pl.multiple_of((1 - core) * half, half), half), :]),
    ]


def block(full, d, mine, width):
    half, quarter = mine.shape[0], full.shape[2]
    return [
        (mine.at[:, width:width + quarter], full.at[d, :half, :]),
        (mine.at[:, width + quarter:], full.at[d, half:, :]),
    ]


def own_f(s, f, quarter):
    at = pl.ds(pl.multiple_of(s[CHIP] * quarter, quarter), quarter)
    return f.at[s[SLOT], :, at]


def split(x):
    high = x.astype(BF)
    return high, (x - high.astype(F32)).astype(BF)


def first_kernel(s, f, own, m1, m2, m3, o1, o2, o3, hi, lo, e, fv, hv, sems):
    span, quarter = fv.shape
    width = e.shape[2]
    pairs = [(own_f(s, f, quarter), fv), (own.at[s[SLOT]], e.at[0])]
    for d, mine, other in ((1, m1, o1), (2, m2, o2), (3, m3, o3)):
        pairs += halves(e, d, mine, other, s[CORE]) + block(hv, d, mine, width)
    fetch(sems, pairs)
    x = mm(fv[...].T.astype(BF), e[0], NN)
    for d in (1, 2, 3):
        x += mm(hv[d].astype(F32).T.astype(BF), e[d], NN)
    high, low = split(x)
    hi[...] = high
    for q in range(4):
        lo[q] = low[:, q * span:(q + 1) * span]


def second_kernel(
    s, f, strips, xp, e, m1, m2, m3, n1, n2, n3, o1, o2, o3, lo_a, hi, lo, w, fv, hv, gv, xv, ev, lv, sems
):
    span, quarter = fv.shape
    width = w.shape[2]
    pairs = [(own_f(s, f, quarter), fv), (xp, xv), (e, ev), (lo_a, lv), (strips.at[0, s[SLOT]], w.at[0])]
    for d, first, mine, other in ((1, m1, n1, o1), (2, m2, n2, o2), (3, m3, n3, o3)):
        pairs += halves(w, d, mine, other, s[CORE])
        pairs += block(hv, d, first, width) + block(gv, d, mine, width)
    fetch(sems, pairs)
    xt = xv[...].astype(F32).T.astype(BF)
    x = jnp.zeros(hi.shape, F32)
    for d in range(4):
        old = fv[...] if d == 0 else hv[d].astype(F32) + gv[d].astype(F32)
        new = old - mm(w[d], xt, NN)
        x += mm(new.T.astype(BF), ev[d], NN)
    high, low = split(x)
    hi[...] = high

    @pl.when(s[IS_A] == 1)
    def _():
        lo[...] = lv[...]

    @pl.when(s[IS_A] == 0)
    def _():
        for q in range(4):
            lo[q] = low[:, q * span:(q + 1) * span]


def third_kernel(s, part, far, e, w, y, r, pv, rv, ev, wv, sems):
    fetch(sems, [(part, pv), (far, rv), (e, ev), (w, wv)])
    rest = ((pv[...] + rv[...]) * (-1.0 / SUM_SCALE)).T.astype(BF)
    back = jnp.zeros(r.shape, F32)
    for d in range(4):
        yq = mm(ev[d], rest, NN)
        y[s[CHIP] ^ d] = yq
        back += mm(yq.T.astype(BF), wv[d], NN)
    r[...] = back


def fourth_kernel(s, part, far, r, e, y_b, y, pv, rv, bv, ev, sems):
    @pl.when(s[IS_A] == 0)
    def _():
        fetch(sems, [(y_b, y)])

    @pl.when(s[IS_A] == 1)
    def _():
        fetch(sems, [(part, pv), (far, rv), (r, bv), (e, ev)])
        rest = ((pv[...] + rv[...]) * (-1.0 / SUM_SCALE) - bv[...]).T.astype(BF)
        for d in range(4):
            y[s[CHIP] ^ d] = mm(ev[d], rest, NN)


def fill(x_full, pieces, chip):
    for d, piece in enumerate(pieces):
        quarter = piece.shape[0]
        at = pl.ds(pl.multiple_of((chip ^ d) * quarter, quarter), quarter)
        x_full[:, at] = piece[...].astype(F32).T.astype(BF)


def update_one_kernel(s, f_ref, w_ref, x0, x1, x2, x3, out_ref, x_full):
    a = pl.program_id(0)

    @pl.when(a == 0)
    def _():
        fill(x_full, (x0, x1, x2, x3), s[CHIP])

    later = 4 * a + s[PLANE] > s[PANEL] + 1

    @pl.when(later)
    def _():
        out_ref[0] = f_ref[0] - mm(w_ref[0, 0], x_full[...], NN)

    @pl.when(jnp.logical_not(later))
    def _():
        out_ref[...] = f_ref[...]


def update_two_kernel(s, f_ref, w_ref, x0, x1, x2, x3, p0, p1, p2, p3, lo_ref, out_ref, x_full):
    a = pl.program_id(0)
    span = f_ref.shape[1]
    quarter = lo_ref.shape[1]
    own = (a == s[SLOT]) & (s[OWNS] == 1)

    @pl.when(a == 0)
    def _():
        fill(x_full, (x0, x1, x2, x3), s[CHIP])

    @pl.when(4 * a + s[PLANE] > s[PANEL] + 1)
    def _():
        out_ref[0] = f_ref[0] - mm(w_ref[0, 0], x_full[...], NN)

    def solved(pieces):
        at = pl.ds(pl.multiple_of(s[CHIP] * span, span), span)
        for d, piece in enumerate(pieces):
            q = s[CHIP] ^ d
            x = piece[:, at].astype(F32) + lo_ref[q].astype(F32)
            out_ref[0, :, pl.ds(pl.multiple_of(q * quarter, quarter), quarter)] = x.T

    @pl.when(own & (s[IS_A] == 1))
    def _():
        solved((p0, p1, p2, p3))

    @pl.when(own & (s[IS_A] == 0))
    def _():
        solved((x0, x1, x2, x3))

    @pl.when((a == s[LOW]) & (4 * a + s[PLANE] <= s[PANEL] + 1) & jnp.logical_not(own))
    def _():
        out_ref[...] = f_ref[...]


def update_one(s, fwd_state, strips, pieces):
    tiles, span, columns = fwd_state.shape
    width = strips.shape[3]
    tile = pl.BlockSpec((1, span, columns), lambda a, s: (a, 0, 0))
    return call(
        update_one_kernel, "update_one", s, (tiles,),
        [tile, pl.BlockSpec((1, 1, span, width), lambda a, s: (0, jnp.maximum(a, s[FIRST]), 0, 0))]
        + [whole(columns // 4, width)] * 4,
        tile, shaped(F32, *fwd_state.shape),
        (fwd_state, strips, *pieces),
        scratch=[pltpu.VMEM((width, columns), BF)],
    )


def update_two(s, state, strips, pieces, pieces_p, lo):
    tiles, span, columns = state.shape
    width = strips.shape[3]
    tile = pl.BlockSpec((1, span, columns), lambda a, s: (jnp.maximum(a, s[LOW]), 0, 0))
    return call(
        update_two_kernel, "update_two", s, (tiles,),
        [tile, pl.BlockSpec((1, 1, span, width), lambda a, s: (1, jnp.maximum(a, s[FIRST]), 0, 0))]
        + [whole(columns // 4, width)] * 8 + [whole(*lo.shape)],
        tile, shaped(F32, *state.shape),
        (state, strips, *pieces, *pieces_p, lo),
        scratch=[pltpu.VMEM((width, columns), BF)],
        aliases={1: 0},
    )


def place_kernel(s, copy_ref, y_ref, out_ref):
    quarter = y_ref.shape[2]

    @pl.when(s[OWNS] == 1)
    def _():
        for q in range(4):
            out_ref[0, :, q * quarter:(q + 1) * quarter] = y_ref[q]

    @pl.when(s[OWNS] == 0)
    def _():
        out_ref[...] = copy_ref[...]


def place(s, copy, y):
    tiles, span, columns = copy.shape
    tile = pl.BlockSpec((1, span, columns), lambda i, s: (s[SLOT], 0, 0))
    return call(
        place_kernel, "place", s, (1,), [tile, whole(*y.shape)], tile,
        shaped(F32, *copy.shape), (copy, y), aliases={1: 0},
    )


def after(x, *waits):
    return lax.optimization_barrier((x,) + waits)[0]


def after_all(xs, *waits):
    return lax.optimization_barrier(tuple(xs) + waits)[:len(xs)]


def plane_body(panel, strips, dinv_rows, fwd_state, back_state):
    tiles, span, columns = fwd_state.shape
    width = strips.shape[3]
    half, quarter = span // 2, columns // 4
    device = lax.axis_index("blk")
    plane, chip, core = device // 4, device % 4, lax.axis_index("rhs")
    start = panel[0]
    home = lax.rem(start, 4)
    is_a = plane == home
    is_b = plane == lax.rem(start + 1, 4)
    groups = [[4 * z + j for j in range(4)] for z in range(4)]

    def exchange(x):
        return lax.all_to_all(x, "blk", 0, 0, axis_index_groups=groups, tiled=True)

    def permute(x, to):
        return lax.ppermute(x, "blk", [(i, to(i)) for i in range(16)])

    def up(x):
        return permute(x, lambda i: (i + 4) % 16)

    def down(x):
        return permute(x, lambda i: (i + 12) % 16)

    def across(x):
        return permute(x, lambda i: i ^ 8)

    def deal(xs):
        return [permute(x, lambda i, d=d: i ^ d) for d, x in zip((1, 2, 3), xs)]

    def gather(x):
        return deal([x] * 3)

    def swap(x):
        return lax.ppermute(x, "rhs", [(0, 1), (1, 0)])

    slot = start // 4 + jnp.where(is_b & (home == 3), 1, 0)
    keep = lax.rem(plane + start + 1, 2) == 0
    first_later = jnp.clip((start + 5 - plane) // 4, 0, tiles - 1)
    low = jnp.minimum(first_later, jnp.where(is_a | is_b, slot, tiles - 1))
    s = scalars([slot, is_a | is_b, start, plane, chip, core, keep, is_a, first_later, low])

    piece = shaped(BF, quarter, width)
    piece32 = shaped(F32, quarter, width)
    lows = shaped(BF, 4, quarter, span)
    matrix = shaped(BF, 4, span, width)
    blocks = shaped(F32, 4, span, quarter)
    blocks16 = shaped(BF, 4, span, quarter)
    own = shaped(F32, span, quarter)

    def small(kernel, name, shapes, arrays, buffers, copies):
        return call(
            kernel, name, s, (1,), [HBM] * len(arrays), [whole(*x.shape) for x in shapes], shapes, arrays,
            scratch=[pltpu.VMEM(x.shape, x.dtype) for x in buffers] + [pltpu.SemaphoreType.DMA((copies,))],
        )

    sent = sums_send(s, strips, back_state).astype(HF)
    got = permute(sent, lambda i: i ^ 4)

    to_e, to_w = prep(s, strips, dinv_rows, fwd_state)
    m = deal(to_e)
    kept, copy = sums_keep(after(s, *to_e), strips, back_state)
    m = list(after_all(m, kept))
    n = deal(after_all(to_w, *m))
    m_other = [swap(x) for x in m]
    hi_p, lo_p, e = small(
        first_kernel, "first", [piece, lows, matrix], (fwd_state, dinv_rows, *m, *m_other), [own, blocks16], 14
    )
    below = up(hi_p)

    pair = (after(kept, hi_p) + got.astype(F32)).astype(HF)
    parts = exchange(pair).reshape(4, quarter, width)

    xp = jnp.where(is_a, hi_p, below)
    xp_far = across(xp)
    n_other = [swap(x) for x in n]
    hi_q, lo, w = small(
        second_kernel, "second", [piece, lows, matrix],
        (fwd_state, strips, xp, e, *m, *n, *n_other, lo_p), [own, blocks16, blocks16, piece, matrix, lows], 23,
    )
    xq = jnp.where(is_b, hi_q, across(hi_q))
    xq = jnp.where(keep, xq, permute(xq, lambda i: i ^ 4))

    part = jnp.sum(after(parts, hi_q).astype(F32), axis=0)
    far = across(part.astype(HF)).astype(F32)
    y_b, r = small(
        third_kernel, "third", [blocks, piece32], (part, far, e, w), [piece32, piece32, matrix, matrix], 4
    )
    r = down(r)

    xp = jnp.where(is_a | is_b, xp, xp_far)
    xp_all = [xp] + gather(xp)
    xq_all = [xq] + gather(xq)
    lo_own = exchange(after(lo, y_b).reshape(columns, span)).reshape(4, quarter, span)
    state = update_one(after(s, y_b), fwd_state, strips, xp_all)

    (y,) = small(
        fourth_kernel, "fourth", [blocks], (part, far, r, e, y_b), [piece32, piece32, piece32, matrix], 4
    )
    y_own = exchange(y.reshape(4 * span, quarter)).reshape(4, span, quarter)
    fwd_out = update_two(after(s, y), state, strips, xq_all, xp_all, lo_own)
    back_out = place(s, copy, y_own)
    return fwd_out, back_out


def body(panel, strips, dinv_rows, fwd_state, back_state):
    tiles, span, columns = fwd_state.shape
    width = strips.shape[3]
    blocks = lax.axis_size("blk")
    regular = (
        blocks == 16
        and lax.axis_size("rhs") == 2
        and width == 4 * span
        and span % 256 == 0
        and columns % 512 == 0
    )
    chosen = plane_body if regular else plain_body
    return chosen(panel, strips, dinv_rows, fwd_state, back_state)


def solution(mesh):
    return jax.shard_map(
        body,
        mesh=mesh,
        in_specs=(
            P(),
            P(None, None, "blk", None),
            P(None, "blk", None),
            P(None, "blk", "rhs"),
            P(None, "blk", "rhs"),
        ),
        out_specs=(P(None, "blk", "rhs"), P(None, "blk", "rhs")),
        check_vma=False,
    )
```

```python
import functools

import jax
import jax.numpy as jnp
from jax import lax
from jax.experimental import pallas as pl
from jax.experimental.pallas import tpu as pltpu
from jax.sharding import PartitionSpec as P

BF = jnp.bfloat16
HF = jnp.float16
F32 = jnp.float32
SUM_SCALE = 4.0
MIB = 1024 * 1024

NN = (((1,), (0,)), ((), ()))


def mm(a, b, dims):
    return lax.dot_general(a, b, dims, preferred_element_type=F32)


def plain_body(panel, strips, dinv_rows, fwd_state, back_state):
    tiles, span, columns = fwd_state.shape
    width = strips.shape[3]
    per_panel = width // span
    blocks = lax.axis_size("blk")
    device = lax.axis_index("blk")
    start = panel[0]
    slots = jnp.arange(tiles, dtype=jnp.int32)
    block_of = (slots * blocks + device) // per_panel

    def locate(k):
        offset = jnp.mod(device - per_panel * k, blocks)
        holds = offset < per_panel
        local = jnp.clip((per_panel * k + offset) // blocks, 0, tiles - 1)
        return (holds, local, jnp.minimum(offset, per_panel - 1))

    def forward(k, which, state):
        holds, local, offset = locate(k)
        strip = strips[which]
        current = lax.dynamic_index_in_dim(state, local, 0, keepdims=False).astype(BF)
        inv_tile = lax.dynamic_index_in_dim(dinv_rows, local, 0, keepdims=False)
        partial_rows = lax.dot_general(
            inv_tile, current, (((0,), (0,)), ((), ())), preferred_element_type=F32
        )
        partial_rows = jnp.where(holds, partial_rows, 0.0)
        later = (block_of > k)[:, None, None]
        solved = lax.psum(partial_rows, "blk")
        delta = jnp.einsum(
            "atw,wc->atc", strip, solved.astype(BF), preferred_element_type=F32
        )
        state = state - jnp.where(later, delta, 0.0)
        own_tile = lax.dynamic_slice_in_dim(solved, offset * span, span, 0)
        placed = lax.dynamic_update_index_in_dim(state, own_tile, local, 0)
        return jnp.where(holds, placed, state)

    def backward(k, which, state):
        holds, local, offset = locate(k)
        strip = strips[which]
        known = jnp.where((block_of > k)[:, None, None], state, 0.0).astype(BF)
        term = -jnp.einsum("atw,atc->wc", strip, known, preferred_element_type=F32)
        current = lax.dynamic_index_in_dim(state, local, 0, keepdims=False)
        placed_rows = lax.dynamic_update_slice_in_dim(
            jnp.zeros((width, columns), F32), current, offset * span, 0
        )
        term = term + jnp.where(holds, placed_rows, 0.0)
        summed = lax.psum(term, "blk").astype(BF)
        inv_tile = lax.dynamic_index_in_dim(dinv_rows, local, 0, keepdims=False)
        solved_tile = jnp.dot(inv_tile, summed, preferred_element_type=F32)
        placed = lax.dynamic_update_index_in_dim(state, solved_tile, local, 0)
        return jnp.where(holds, placed, state)

    fwd_out = forward(start, 0, fwd_state)
    fwd_out = forward(start + 1, 1, fwd_out)
    back_out = backward(start + 1, 1, back_state)
    back_out = backward(start, 0, back_out)
    return (fwd_out, back_out)


SLOT, OWNS, PANEL, PLANE, CHIP, CORE, KEEP, IS_A, FIRST, LOW = range(10)


def scalars(values):
    lane = lax.broadcasted_iota(jnp.int32, (16,), 0)
    out = jnp.zeros((16,), jnp.int32)
    for i, value in enumerate(values):
        out = jnp.where(lane == i, value.astype(jnp.int32), out)
    return out


def call(kernel, name, s, grid, ins, outs, shapes, arrays, scratch=(), aliases=None, limit=63):
    return pl.pallas_call(
        kernel,
        grid_spec=pltpu.PrefetchScalarGridSpec(
            num_scalar_prefetch=1, grid=grid, in_specs=ins, out_specs=outs, scratch_shapes=list(scratch)
        ),
        out_shape=shapes,
        input_output_aliases=aliases or {},
        compiler_params=pltpu.CompilerParams(vmem_limit_bytes=limit * MIB),
        name=name,
    )(s, *arrays)


def whole(*shape):
    return pl.BlockSpec(shape, lambda i, s: (0,) * len(shape), pipeline_mode=pl.Buffered(1))


def shaped(dtype, *shape):
    return jax.ShapeDtypeStruct(shape, dtype)


def prep_kernel(s, e_ref, w_ref, f_ref, *outs):
    half, width = e_ref.shape[1:]
    quarter = (outs[0].shape[1] - width) // 2
    for d in (1, 2, 3):
        at = pl.ds(pl.multiple_of((s[CHIP] ^ d) * quarter, quarter), quarter)
        high, low = split(f_ref[0, :, at])
        for out, matrix, f in ((outs[d - 1], e_ref[0], high), (outs[d + 2], w_ref[0, 0], low)):
            out[:, :width] = matrix
            out[:, width:width + quarter] = f[:half]
            out[:, width + quarter:] = f[half:]


def prep(s, strips, dinv_rows, fwd_state):
    tiles, span, columns = fwd_state.shape
    width = strips.shape[3]
    half, quarter = span // 2, columns // 4
    outs = call(
        prep_kernel, "prep", s, (1,),
        [
            pl.BlockSpec((1, half, width), lambda i, s: (s[SLOT], s[CORE], 0)),
            pl.BlockSpec((1, 1, half, width), lambda i, s: (0, s[SLOT], s[CORE], 0)),
            pl.BlockSpec((1, span, columns), lambda i, s: (s[SLOT], 0, 0)),
        ],
        [whole(half, width + 2 * quarter)] * 6,
        [shaped(BF, half, width + 2 * quarter)] * 6,
        (dinv_rows, strips, fwd_state),
    )
    return outs[:3], outs[3:]


def later(s, slot):
    return 4 * slot + s[PLANE] > s[PANEL] + 1


def sums_kernel(own, s, w_ref, b_ref, out_ref, *copies):
    a = pl.program_id(0)
    _, span, columns = b_ref.shape

    @pl.when(a == 0)
    def _():
        out_ref[...] = jnp.zeros_like(out_ref)

    for copy in copies:
        copy[...] = b_ref[...]

    @pl.when(later(s, 2 * a + 1))
    def _():
        b = b_ref[...].reshape(2 * span, columns) * SUM_SCALE
        row = lax.broadcasted_iota(jnp.int32, b.shape, 0)
        b = jnp.where((row >= span) | later(s, 2 * a), b, 0.0)
        out_ref[...] += mm(b.T.astype(BF), w_ref[0].reshape(2 * span, -1), NN)

    if own:
        @pl.when((a == s[SLOT] // 2) & (s[OWNS] == 1))
        def _():
            at = pl.ds(pl.multiple_of(s[CHIP] * span, span), span)
            out_ref[:, at] = out_ref[:, at] - (b_ref[s[SLOT] % 2] * SUM_SCALE).T


def sums(s, own, strips, back_state):
    tiles, span, columns = back_state.shape
    width = strips.shape[3]

    def which(s):
        return s[KEEP] if own else 1 - s[KEEP]

    def at(a, s):
        return jnp.maximum(a, s[FIRST] // 2)

    tile = pl.BlockSpec((2, span, columns), lambda a, s: (a if own else at(a, s), 0, 0))
    return call(
        functools.partial(sums_kernel, own), "sums", s, (tiles // 2,),
        [pl.BlockSpec((1, 2, span, width), lambda a, s: (which(s), at(a, s), 0, 0)), tile],
        [whole(columns, width)] + [tile] * own,
        [shaped(F32, columns, width)] + [shaped(F32, *back_state.shape)] * own,
        (strips, back_state),
    )


HBM = pl.BlockSpec(memory_space=pltpu.HBM)


def fetch(sems, pairs):
    copies = [pltpu.make_async_copy(a, b, sems.at[i]) for i, (a, b) in enumerate(pairs)]
    for copy in copies:
        copy.start()
    for copy in copies:
        copy.wait()


def halves(full, d, mine, other, core):
    half, width = mine.shape[0], full.shape[2]
    return [
        (mine.at[:, :width], full.at[d, pl.ds(pl.multiple_of(core * half, half), half), :]),
        (other.at[:, :width], full.at[d, pl.ds(pl.multiple_of((1 - core) * half, half), half), :]),
    ]


def block(full, d, mine, width):
    half, quarter = mine.shape[0], full.shape[2]
    return [
        (mine.at[:, width:width + quarter], full.at[d, :half, :]),
        (mine.at[:, width + quarter:], full.at[d, half:, :]),
    ]


def own_f(s, f, quarter):
    at = pl.ds(pl.multiple_of(s[CHIP] * quarter, quarter), quarter)
    return f.at[s[SLOT], :, at]


def split(x):
    high = x.astype(BF)
    return high, (x - high.astype(F32)).astype(BF)


def first_kernel(s, f, own, m1, m2, m3, o1, o2, o3, hi, lo, e, fv, hv, sems):
    _, quarter = fv.shape
    width = e.shape[2]
    pairs = [(own_f(s, f, quarter), fv), (own.at[s[SLOT]], e.at[0])]
    for d, mine, other in ((1, m1, o1), (2, m2, o2), (3, m3, o3)):
        pairs += halves(e, d, mine, other, s[CORE]) + block(hv, d, mine, width)
    fetch(sems, pairs)
    x = mm(fv[...].T.astype(BF), e[0], NN)
    for d in (1, 2, 3):
        x += mm(hv[d].astype(F32).T.astype(BF), e[d], NN)
    hi[...], lo[...] = split(x.T)


def second_kernel(
    s, f, strips, xp, e, m1, m2, m3, n1, n2, n3, o1, o2, o3, lo_a, hi, lo, w, fv, hv, gv, xv, ev, lv, sems
):
    _, quarter = fv.shape
    width = w.shape[2]
    pairs = [(own_f(s, f, quarter), fv), (xp, xv), (e, ev), (lo_a, lv), (strips.at[0, s[SLOT]], w.at[0])]
    for d, first, mine, other in ((1, m1, n1, o1), (2, m2, n2, o2), (3, m3, n3, o3)):
        pairs += halves(w, d, mine, other, s[CORE])
        pairs += block(hv, d, first, width) + block(gv, d, mine, width)
    fetch(sems, pairs)
    x = jnp.zeros((quarter, width), F32)
    for d in range(4):
        old = fv[...] if d == 0 else hv[d].astype(F32) + gv[d].astype(F32)
        new = old - mm(w[d], xv[...], NN)
        x += mm(new.T.astype(BF), ev[d], NN)
    high, low = split(x.T)
    hi[...] = high

    @pl.when(s[IS_A] == 1)
    def _():
        lo[...] = lv[...]

    @pl.when(s[IS_A] == 0)
    def _():
        lo[...] = low


def third_kernel(s, part, far, e, w, y, r, pv, rv, ev, wv, sems):
    fetch(sems, [(part, pv), (far, rv), (e, ev), (w, wv)])
    rest = ((pv[...] + rv[...]) * (-1.0 / SUM_SCALE)).T.astype(BF)
    back = jnp.zeros(r.shape, F32)
    for d in range(4):
        yq = mm(ev[d], rest, NN)
        y[s[CHIP] ^ d] = yq
        back += mm(yq.T.astype(BF), wv[d], NN)
    r[...] = back


def fourth_kernel(s, part, far, r, e, y_b, y, pv, rv, bv, ev, sems):
    @pl.when(s[IS_A] == 0)
    def _():
        fetch(sems, [(y_b, y)])

    @pl.when(s[IS_A] == 1)
    def _():
        fetch(sems, [(part, pv), (far, rv), (r, bv), (e, ev)])
        rest = ((pv[...] + rv[...]) * (-1.0 / SUM_SCALE) - bv[...]).T.astype(BF)
        for d in range(4):
            y[s[CHIP] ^ d] = mm(ev[d], rest, NN)


def fill(x_full, pieces, chip):
    for d, piece in enumerate(pieces):
        quarter = piece.shape[1]
        x_full[:, pl.ds(pl.multiple_of((chip ^ d) * quarter, quarter), quarter)] = piece[...]


def subtract(s, a, f_ref, w_ref, x_full, out_ref):
    _, span, width = w_ref.shape[1:]
    delta = mm(w_ref[0].reshape(2 * span, width), x_full[...], NN)
    for j in range(2):
        rest = f_ref[j] - delta[j * span:(j + 1) * span]
        out_ref[j] = jnp.where(later(s, 2 * a + j), rest, f_ref[j])


def update_one_kernel(s, f_ref, w_ref, x0, x1, x2, x3, out_ref, x_full):
    a = pl.program_id(0)

    @pl.when(a == 0)
    def _():
        fill(x_full, (x0, x1, x2, x3), s[CHIP])

    @pl.when(later(s, 2 * a + 1))
    def _():
        subtract(s, a, f_ref, w_ref, x_full, out_ref)

    @pl.when(jnp.logical_not(later(s, 2 * a + 1)))
    def _():
        out_ref[...] = f_ref[...]


def update_two_kernel(s, f_ref, w_ref, x0, x1, x2, x3, p0, p1, p2, p3, lo_ref, out_ref, x_full):
    a = pl.program_id(0)
    span = f_ref.shape[1]
    quarter = lo_ref.shape[2]

    @pl.when(a == 0)
    def _():
        fill(x_full, (x0, x1, x2, x3), s[CHIP])

    @pl.when(later(s, 2 * a + 1))
    def _():
        subtract(s, a, f_ref, w_ref, x_full, out_ref)

    @pl.when((a == s[LOW]) & jnp.logical_not(later(s, 2 * a + 1)))
    def _():
        out_ref[...] = f_ref[...]

    def solved(pieces):
        at = pl.ds(pl.multiple_of(s[CHIP] * span, span), span)
        for d, piece in enumerate(pieces):
            q = s[CHIP] ^ d
            x = piece[at, :].astype(F32) + lo_ref[q].astype(F32)
            out_ref[s[SLOT] % 2, :, pl.ds(pl.multiple_of(q * quarter, quarter), quarter)] = x

    own = (a == s[SLOT] // 2) & (s[OWNS] == 1)

    @pl.when(own & (s[IS_A] == 1))
    def _():
        solved((p0, p1, p2, p3))

    @pl.when(own & (s[IS_A] == 0))
    def _():
        solved((x0, x1, x2, x3))


def update(kernel, which, low, s, state, strips, pieces, own=(), aliases=None):
    tiles, span, columns = state.shape
    width = strips.shape[3]
    tile = pl.BlockSpec((2, span, columns), lambda a, s: (jnp.maximum(a, low(s)), 0, 0))
    return call(
        kernel, "update", s, (tiles // 2,),
        [tile, pl.BlockSpec((1, 2, span, width), lambda a, s: (which, jnp.maximum(a, s[FIRST] // 2), 0, 0))]
        + [whole(*x.shape) for x in (*pieces, *own)],
        tile, shaped(F32, *state.shape),
        (state, strips, *pieces, *own),
        scratch=[pltpu.VMEM((width, columns), BF)],
        aliases=aliases,
    )


def place_kernel(s, copy_ref, y_ref, out_ref):
    quarter = y_ref.shape[2]

    @pl.when(s[OWNS] == 1)
    def _():
        for q in range(4):
            out_ref[0, :, q * quarter:(q + 1) * quarter] = y_ref[q]

    @pl.when(s[OWNS] == 0)
    def _():
        out_ref[...] = copy_ref[...]


def place(s, copy, y):
    tiles, span, columns = copy.shape
    tile = pl.BlockSpec((1, span, columns), lambda i, s: (s[SLOT], 0, 0))
    return call(
        place_kernel, "place", s, (1,), [tile, whole(*y.shape)], tile,
        shaped(F32, *copy.shape), (copy, y), aliases={1: 0},
    )


def after(x, *waits):
    return lax.optimization_barrier((x,) + waits)[0]


def after_all(xs, *waits):
    return lax.optimization_barrier(tuple(xs) + waits)[:len(xs)]


def plane_body(panel, strips, dinv_rows, fwd_state, back_state):
    tiles, span, columns = fwd_state.shape
    width = strips.shape[3]
    half, quarter = span // 2, columns // 4
    device = lax.axis_index("blk")
    plane, chip, core = device // 4, device % 4, lax.axis_index("rhs")
    start = panel[0]
    home = lax.rem(start, 4)
    is_a = plane == home
    is_b = plane == lax.rem(start + 1, 4)
    groups = [[4 * z + j for j in range(4)] for z in range(4)]

    def exchange(x):
        return lax.all_to_all(x, "blk", 0, 0, axis_index_groups=groups, tiled=True)

    def permute(x, to):
        return lax.ppermute(x, "blk", [(i, to(i)) for i in range(16)])

    def up(x):
        return permute(x, lambda i: (i + 4) % 16)

    def down(x):
        return permute(x, lambda i: (i + 12) % 16)

    def across(x):
        return permute(x, lambda i: i ^ 8)

    def deal(xs):
        return [permute(x, lambda i, d=d: i ^ d) for d, x in zip((1, 2, 3), xs)]

    def gather(x):
        return deal([x] * 3)

    def swap(x):
        return lax.ppermute(x, "rhs", [(0, 1), (1, 0)])

    slot = start // 4 + jnp.where(is_b & (home == 3), 1, 0)
    first_later = jnp.clip((start + 5 - plane) // 4, 0, tiles - 1)
    low = jnp.minimum(first_later, jnp.where(is_a | is_b, slot, tiles - 1)) // 2
    keep = lax.rem(plane + start + 1, 2) == 0
    s = scalars([slot, is_a | is_b, start, plane, chip, core, keep, is_a, first_later, low])

    piece = shaped(BF, width, quarter)
    piece32 = shaped(F32, quarter, width)
    matrix = shaped(BF, 4, span, width)
    blocks = shaped(F32, 4, span, quarter)
    blocks16 = shaped(BF, 4, span, quarter)
    own = shaped(F32, span, quarter)

    def small(kernel, name, shapes, arrays, buffers, copies):
        return call(
            kernel, name, s, (1,), [HBM] * len(arrays), [whole(*x.shape) for x in shapes], shapes, arrays,
            scratch=[pltpu.VMEM(x.shape, x.dtype) for x in buffers] + [pltpu.SemaphoreType.DMA((copies,))],
        )

    (sent,) = sums(s, 0, strips, back_state)
    sent = sent.astype(HF)
    got = permute(sent, lambda i: i ^ 4)

    to_e, to_w = prep(after(s, sent), strips, dinv_rows, fwd_state)
    m = deal(to_e)
    kept, copy = sums(after(s, *to_e), 1, strips, back_state)
    m = after_all(m, kept)
    m_other = [swap(x) for x in m]
    n = deal(to_w)
    hi_p, lo_p, e = small(
        first_kernel, "first", [piece, piece, matrix], (fwd_state, dinv_rows, *m, *m_other), [own, blocks16], 14
    )
    below = up(hi_p)

    pair = (after(kept, hi_p) + got.astype(F32)).astype(HF)
    parts = exchange(pair).reshape(4, quarter, width)

    xp = jnp.where(is_a, hi_p, below)
    xp_far = across(xp)
    n_other = [swap(x) for x in n]
    hi_q, lo, w = small(
        second_kernel, "second", [piece, piece, matrix],
        (fwd_state, strips, xp, e, *m, *n, *n_other, lo_p), [own, blocks16, blocks16, piece, matrix, piece], 23,
    )
    part = jnp.sum(parts.astype(F32), axis=0)
    part16 = part.astype(HF)

    def last(first):
        source = (first + 1) % 4

        def send(x, *pairs):
            return lax.ppermute(x, "blk", [(4 * a + j, 4 * b + j) for a, b in pairs for j in range(4)])

        def run(x, xp, part):
            far = send(part, (first ^ 2, first), (source ^ 2, source))
            got = [send(x, (source, z)) for z in range(4) if z != source]
            return jnp.where(is_b, x, sum(got)), gather(xp), far.astype(F32)

        return run

    xp = jnp.where(is_a | is_b, xp, xp_far)
    xq, xp_rest, far = lax.switch(home, [last(z) for z in range(4)], hi_q, xp, part16)
    xp_all = [xp] + xp_rest
    xq_all = [xq] + gather(xq)

    y_b, r = small(
        third_kernel, "third", [blocks, piece32], (part, far, e, w),
        [piece32, piece32, matrix, matrix], 4,
    )
    r = down(r)
    lo_own = exchange(after(lo, y_b)).reshape(4, span, quarter)
    state = update(update_one_kernel, 0, lambda s: 0, after(s, y_b), fwd_state, strips, xp_all)
    (y,) = small(
        fourth_kernel, "fourth", [blocks], (part, far, r, e, after(y_b, state, *xq_all)),
        [piece32, piece32, piece32, matrix], 4,
    )
    y_own = exchange(y.reshape(4 * span, quarter)).reshape(4, span, quarter)
    fwd_out = update(
        update_two_kernel, 1, lambda s: s[LOW], after(s, y), state, strips, xq_all, (*xp_all, lo_own), {1: 0}
    )
    back_out = place(s, copy, y_own)
    return fwd_out, back_out


def body(panel, strips, dinv_rows, fwd_state, back_state):
    tiles, span, columns = fwd_state.shape
    width = strips.shape[3]
    blocks = lax.axis_size("blk")
    regular = (
        blocks == 16
        and lax.axis_size("rhs") == 2
        and width == 4 * span
        and span % 256 == 0
        and columns % 512 == 0
        and tiles % 2 == 0
    )
    chosen = plane_body if regular else plain_body
    return chosen(panel, strips, dinv_rows, fwd_state, back_state)


def solution(mesh):
    return jax.shard_map(
        body,
        mesh=mesh,
        in_specs=(
            P(),
            P(None, None, "blk", None),
            P(None, "blk", None),
            P(None, "blk", "rhs"),
            P(None, "blk", "rhs"),
        ),
        out_specs=(P(None, "blk", "rhs"), P(None, "blk", "rhs")),
        check_vma=False,
    )
```

```python
import functools

import jax
import jax.numpy as jnp
from jax import lax
from jax.experimental import pallas as pl
from jax.experimental.pallas import tpu as pltpu
from jax.sharding import PartitionSpec as P

BF = jnp.bfloat16
HF = jnp.float16
F32 = jnp.float32
SUM_SCALE = 4.0
MIB = 1024 * 1024

NN = (((1,), (0,)), ((), ()))


def mm(a, b, dims):
    return lax.dot_general(a, b, dims, preferred_element_type=F32)


def plain_body(panel, strips, dinv_rows, fwd_state, back_state):
    tiles, span, columns = fwd_state.shape
    width = strips.shape[3]
    per_panel = width // span
    blocks = lax.axis_size("blk")
    device = lax.axis_index("blk")
    start = panel[0]
    slots = jnp.arange(tiles, dtype=jnp.int32)
    block_of = (slots * blocks + device) // per_panel

    def locate(k):
        offset = jnp.mod(device - per_panel * k, blocks)
        holds = offset < per_panel
        local = jnp.clip((per_panel * k + offset) // blocks, 0, tiles - 1)
        return (holds, local, jnp.minimum(offset, per_panel - 1))

    def forward(k, which, state):
        holds, local, offset = locate(k)
        strip = strips[which]
        current = lax.dynamic_index_in_dim(state, local, 0, keepdims=False).astype(BF)
        inv_tile = lax.dynamic_index_in_dim(dinv_rows, local, 0, keepdims=False)
        partial_rows = lax.dot_general(
            inv_tile, current, (((0,), (0,)), ((), ())), preferred_element_type=F32
        )
        partial_rows = jnp.where(holds, partial_rows, 0.0)
        later = (block_of > k)[:, None, None]
        solved = lax.psum(partial_rows, "blk")
        delta = jnp.einsum(
            "atw,wc->atc", strip, solved.astype(BF), preferred_element_type=F32
        )
        state = state - jnp.where(later, delta, 0.0)
        own_tile = lax.dynamic_slice_in_dim(solved, offset * span, span, 0)
        placed = lax.dynamic_update_index_in_dim(state, own_tile, local, 0)
        return jnp.where(holds, placed, state)

    def backward(k, which, state):
        holds, local, offset = locate(k)
        strip = strips[which]
        known = jnp.where((block_of > k)[:, None, None], state, 0.0).astype(BF)
        term = -jnp.einsum("atw,atc->wc", strip, known, preferred_element_type=F32)
        current = lax.dynamic_index_in_dim(state, local, 0, keepdims=False)
        placed_rows = lax.dynamic_update_slice_in_dim(
            jnp.zeros((width, columns), F32), current, offset * span, 0
        )
        term = term + jnp.where(holds, placed_rows, 0.0)
        summed = lax.psum(term, "blk").astype(BF)
        inv_tile = lax.dynamic_index_in_dim(dinv_rows, local, 0, keepdims=False)
        solved_tile = jnp.dot(inv_tile, summed, preferred_element_type=F32)
        placed = lax.dynamic_update_index_in_dim(state, solved_tile, local, 0)
        return jnp.where(holds, placed, state)

    fwd_out = forward(start, 0, fwd_state)
    fwd_out = forward(start + 1, 1, fwd_out)
    back_out = backward(start + 1, 1, back_state)
    back_out = backward(start, 0, back_out)
    return (fwd_out, back_out)


SLOT, OWNS, PANEL, PLANE, CHIP, CORE, KEEP, IS_A = range(8)


def scalars(values):
    lane = lax.broadcasted_iota(jnp.int32, (16,), 0)
    out = jnp.zeros((16,), jnp.int32)
    for i, value in enumerate(values):
        out = jnp.where(lane == i, value.astype(jnp.int32), out)
    return out


def call(kernel, name, s, grid, ins, outs, shapes, arrays, scratch=(), aliases=None, limit=63):
    return pl.pallas_call(
        kernel,
        grid_spec=pltpu.PrefetchScalarGridSpec(
            num_scalar_prefetch=1, grid=grid, in_specs=ins, out_specs=outs, scratch_shapes=list(scratch)
        ),
        out_shape=shapes,
        input_output_aliases=aliases or {},
        compiler_params=pltpu.CompilerParams(vmem_limit_bytes=limit * MIB),
        name=name,
    )(s, *arrays)


HBM = pl.BlockSpec(memory_space=pltpu.HBM)


def whole(*shape):
    return pl.BlockSpec(shape, lambda i, s: (0,) * len(shape), pipeline_mode=pl.Buffered(1))


def shaped(dtype, *shape):
    return jax.ShapeDtypeStruct(shape, dtype)


def prep_kernel(s, e_ref, w_ref, f_ref, *outs):
    half, width = e_ref.shape[1:]
    quarter = (outs[0].shape[1] - width) // 2
    for d in (1, 2, 3):
        at = pl.ds(pl.multiple_of((s[CHIP] ^ d) * quarter, quarter), quarter)
        high, low = split(f_ref[0, :, at])
        for out, matrix, f in ((outs[d - 1], e_ref[0], high), (outs[d + 2], w_ref[0, 0], low)):
            out[:, :width] = matrix
            out[:, width:width + quarter] = f[:half]
            out[:, width + quarter:] = f[half:]


def prep(s, strips, dinv_rows, fwd_state):
    tiles, span, columns = fwd_state.shape
    width = strips.shape[3]
    half, quarter = span // 2, columns // 4
    outs = call(
        prep_kernel, "prep", s, (1,),
        [
            pl.BlockSpec((1, half, width), lambda i, s: (s[SLOT], s[CORE], 0)),
            pl.BlockSpec((1, 1, half, width), lambda i, s: (0, s[SLOT], s[CORE], 0)),
            pl.BlockSpec((1, span, columns), lambda i, s: (s[SLOT], 0, 0)),
        ],
        [whole(half, width + 2 * quarter)] * 6,
        [shaped(BF, half, width + 2 * quarter)] * 6,
        (dinv_rows, strips, fwd_state),
    )
    return outs[:3], outs[3:]


def later(s, slot):
    return 4 * slot + s[PLANE] > s[PANEL] + 1


def sums_kernel(own, s, strips, state, out_ref, *rest):
    copies, (bv, wv, sb, sw, so) = rest[:own], rest[own:]
    tiles, span, _ = bv.shape
    which = s[KEEP] if own else 1 - s[KEEP]

    def rows(a):
        return pltpu.make_async_copy(state.at[a], bv.at[a], sb.at[a])

    def strip(a):
        return pltpu.make_async_copy(strips.at[which, a], wv.at[a], sw.at[a])

    def back(a):
        return pltpu.make_async_copy(bv.at[a], copies[0].at[a], so.at[a])

    for a in range(tiles):
        if own:
            rows(a).start()

        @pl.when(later(s, a))
        def _(a=a):
            if not own:
                rows(a).start()
            strip(a).start()

    out_ref[...] = jnp.zeros_like(out_ref)
    for a in range(tiles):
        if own:
            rows(a).wait()
            back(a).start()

        @pl.when(later(s, a))
        def _(a=a):
            if not own:
                rows(a).wait()
            strip(a).wait()
            out_ref[...] += mm((bv[a] * SUM_SCALE).T.astype(BF), wv[a], NN)

    if own:
        @pl.when(s[OWNS] == 1)
        def _():
            at = pl.ds(pl.multiple_of(s[CHIP] * span, span), span)
            out_ref[:, at] = out_ref[:, at] - (bv[s[SLOT]] * SUM_SCALE).T

        for a in range(tiles):
            back(a).wait()


def sums(s, own, strips, back_state):
    tiles, span, columns = back_state.shape
    width = strips.shape[3]
    return call(
        functools.partial(sums_kernel, own), "sums", s, (1,),
        [HBM] * 2,
        [whole(columns, width)] + [HBM] * own,
        [shaped(F32, columns, width)] + [shaped(F32, *back_state.shape)] * own,
        (strips, back_state),
        scratch=[pltpu.VMEM((tiles, span, columns), F32), pltpu.VMEM((tiles, span, width), BF)]
        + [pltpu.SemaphoreType.DMA((tiles,))] * 3,
    )


def begin(sems, pairs):
    copies = [pltpu.make_async_copy(a, b, sems.at[i]) for i, (a, b) in enumerate(pairs)]
    for copy in copies:
        copy.start()
    return copies


def finish(copies):
    for copy in copies:
        copy.wait()


def fetch(sems, pairs):
    finish(begin(sems, pairs))


def halves(full, d, mine, other, core):
    half, width = mine.shape[0], full.shape[2]
    return [
        (mine.at[:, :width], full.at[d, pl.ds(pl.multiple_of(core * half, half), half), :]),
        (other.at[:, :width], full.at[d, pl.ds(pl.multiple_of((1 - core) * half, half), half), :]),
    ]


def block(full, d, mine, width):
    half, quarter = mine.shape[0], full.shape[2]
    return [
        (mine.at[:, width:width + quarter], full.at[d, :half, :]),
        (mine.at[:, width + quarter:], full.at[d, half:, :]),
    ]


def own_f(s, f, quarter):
    at = pl.ds(pl.multiple_of(s[CHIP] * quarter, quarter), quarter)
    return f.at[s[SLOT], :, at]


def split(x):
    high = x.astype(BF)
    return high, (x - high.astype(F32)).astype(BF)


def first_kernel(s, f, own, m1, m2, m3, o1, o2, o3, hi, lo, e, fv, hv, sems):
    _, quarter = fv.shape
    width = e.shape[2]
    pairs = [(own_f(s, f, quarter), fv), (own.at[s[SLOT]], e.at[0])]
    for d, mine, other in ((1, m1, o1), (2, m2, o2), (3, m3, o3)):
        pairs += halves(e, d, mine, other, s[CORE]) + block(hv, d, mine, width)
    copies = begin(sems, pairs)
    finish(copies[:2])
    x = mm(fv[...].T.astype(BF), e[0], NN)
    for d in (1, 2, 3):
        finish(copies[4 * d - 2:4 * d + 2])
        x += mm(hv[d].astype(F32).T.astype(BF), e[d], NN)
    hi[...], lo[...] = split(x.T)


def second_kernel(
    s, f, strips, xp, e, m1, m2, m3, n1, n2, n3, o1, o2, o3, lo_a, hi, lo, fv, hv, gv, xv, ev, wv, lv, sems
):
    _, quarter = fv.shape
    width = wv.shape[2]
    pairs = [(xp, xv), (own_f(s, f, quarter), fv), (strips.at[0, s[SLOT]], wv.at[0]), (e.at[0], ev.at[0])]
    for d, first, mine, other in ((1, m1, n1, o1), (2, m2, n2, o2), (3, m3, n3, o3)):
        pairs += halves(wv, d, mine, other, s[CORE])
        pairs += block(hv, d, first, width) + block(gv, d, mine, width) + [(e.at[d], ev.at[d])]
    pairs += [(lo_a, lv)]
    copies = begin(sems, pairs)
    x = jnp.zeros((quarter, width), F32)
    for d in range(4):
        finish(copies[:4] if d == 0 else copies[7 * d - 3:7 * d + 4])
        old = fv[...] if d == 0 else hv[d].astype(F32) + gv[d].astype(F32)
        new = old - mm(wv[d], xv[...], NN)
        x += mm(new.T.astype(BF), ev[d], NN)
    high, low = split(x.T)
    hi[...] = high
    finish(copies[25:])

    @pl.when(s[IS_A] == 1)
    def _():
        lo[...] = lv[...]

    @pl.when(s[IS_A] == 0)
    def _():
        lo[...] = low


def third_kernel(s, part, far, e, strips, n1, n2, n3, o1, o2, o3, y, r, pv, rv, ev, wv, sems):
    pairs = [(part, pv), (far, rv), (e.at[0], ev.at[0]), (strips.at[0, s[SLOT]], wv.at[0])]
    for d, mine, other in ((1, n1, o1), (2, n2, o2), (3, n3, o3)):
        pairs += halves(wv, d, mine, other, s[CORE]) + [(e.at[d], ev.at[d])]
    copies = begin(sems, pairs)
    finish(copies[:2])
    rest = ((pv[...] + rv[...]) * (-1.0 / SUM_SCALE)).T.astype(BF)
    back = jnp.zeros(r.shape, F32)
    for d in range(4):
        finish(copies[2:4] if d == 0 else copies[3 * d + 1:3 * d + 4])
        yq = mm(ev[d], rest, NN)
        y[d] = yq
        back += mm(yq.T.astype(BF), wv[d], NN)
    r[...] = back


def fourth_kernel(s, part, far, r, e, y_b, y0, y1, y2, y3, pv, rv, bv, ev, sems):
    outs = (y0, y1, y2, y3)

    @pl.when(s[IS_A] == 0)
    def _():
        fetch(sems, [(y_b.at[d], y) for d, y in enumerate(outs)])

    @pl.when(s[IS_A] == 1)
    def _():
        copies = begin(sems, [(part, pv), (far, rv), (r, bv)] + [(e.at[d], ev.at[d]) for d in range(4)])
        finish(copies[:3])
        rest = ((pv[...] + rv[...]) * (-1.0 / SUM_SCALE) - bv[...]).T.astype(BF)
        for d, y in enumerate(outs):
            finish(copies[3 + d:4 + d])
            y[...] = mm(ev[d], rest, NN)


def gathered(s, x_full, pieces):
    quarter = pieces[0].shape[1]
    return [
        (x, x_full.at[:, pl.ds(pl.multiple_of((s[CHIP] ^ d) * quarter, quarter), quarter)])
        for d, x in enumerate(pieces)
    ]


def update_one_kernel(s, f, strips, x0, x1, x2, x3, out, fv, wv, xv, sf, sw, so, sx):
    tiles = fv.shape[0]

    def state(a):
        return pltpu.make_async_copy(f.at[a], fv.at[a], sf.at[a])

    def strip(a):
        return pltpu.make_async_copy(strips.at[0, a], wv.at[a], sw.at[a])

    def back(a):
        return pltpu.make_async_copy(fv.at[a], out.at[a], so.at[a])

    x = begin(sx, gathered(s, xv, (x0, x1, x2, x3)))
    for a in range(tiles):
        state(a).start()
        pl.when(later(s, a))(strip(a).start)
    finish(x)
    for a in range(tiles):
        state(a).wait()

        @pl.when(later(s, a))
        def _(a=a):
            strip(a).wait()
            fv[a] = fv[a] - mm(wv[a], xv[...], NN)

        back(a).start()
    for a in range(tiles):
        back(a).wait()


def update_two_kernel(
    s, f, strips, x0, x1, x2, x3, p0, p1, p2, p3, lo, out, fv, wv, xv, sf, sw, so, sx, pv, lv, sp
):
    tiles, span, columns = fv.shape
    quarter = columns // 4
    rows = pl.ds(pl.multiple_of(s[CHIP] * span, span), span)

    def state(a):
        return pltpu.make_async_copy(f.at[a], fv.at[a], sf.at[a])

    def strip(a):
        return pltpu.make_async_copy(strips.at[1, a], wv.at[a], sw.at[a])

    def back(a):
        return pltpu.make_async_copy(fv.at[a], out.at[a], so.at[a])

    x = begin(sx, gathered(s, xv, (x0, x1, x2, x3)))
    for a in range(tiles):
        @pl.when(later(s, a))
        def _(a=a):
            state(a).start()
            strip(a).start()

    own = begin(sp, gathered(s, pv, [p.at[rows, :] for p in (p0, p1, p2, p3)]) + [(lo, lv)])
    finish(x)
    for a in range(tiles):
        @pl.when(later(s, a))
        def _(a=a):
            state(a).wait()
            strip(a).wait()
            fv[a] = fv[a] - mm(wv[a], xv[...], NN)
            back(a).start()

    finish(own)
    for a in range(tiles):
        @pl.when((s[SLOT] == a) & (s[OWNS] == 1))
        def _(a=a):
            solved = jnp.where(s[IS_A] == 1, pv[...].astype(F32), xv[rows, :].astype(F32))
            for q in range(4):
                at = slice(q * quarter, (q + 1) * quarter)
                fv[a, :, at] = solved[:, at] + lv[q].astype(F32)
            back(a).start()
            back(a).wait()

        @pl.when(later(s, a))
        def _(a=a):
            back(a).wait()


def update(kernel, s, state, strips, pieces, own=(), aliases=None):
    tiles, span, columns = state.shape
    width = strips.shape[3]
    dma = pltpu.SemaphoreType.DMA
    more = []
    if own:
        more = [pltpu.VMEM((span, columns), BF), pltpu.VMEM(own[-1].shape, BF), dma((5,))]
    return call(
        kernel, "update", s, (1,), [HBM] * (2 + len(pieces) + len(own)), HBM, shaped(F32, *state.shape),
        (state, strips, *pieces, *own),
        scratch=[
            pltpu.VMEM(state.shape, F32), pltpu.VMEM(strips.shape[1:], BF), pltpu.VMEM((width, columns), BF),
            dma((tiles,)), dma((tiles,)), dma((tiles,)), dma((4,)),
        ] + more,
        aliases=aliases,
    )


def place_kernel(s, copy, y0, y1, y2, y3, out, tile, sems):
    @pl.when(s[OWNS] == 1)
    def _():
        fetch(sems, gathered(s, tile, (y0, y1, y2, y3)))
        fetch(sems, [(tile, out.at[s[SLOT]])])


def place(s, copy, pieces):
    _, span, columns = copy.shape
    return call(
        place_kernel, "place", s, (1,), [HBM] * 5, HBM, shaped(F32, *copy.shape), (copy, *pieces),
        scratch=[pltpu.VMEM((span, columns), F32), pltpu.SemaphoreType.DMA((4,))],
        aliases={1: 0}, limit=8,
    )


def after(x, *waits):
    return lax.optimization_barrier((x,) + waits)[0]


def after_all(xs, *waits):
    return lax.optimization_barrier(tuple(xs) + waits)[:len(xs)]


def plane_body(panel, strips, dinv_rows, fwd_state, back_state):
    tiles, span, columns = fwd_state.shape
    width = strips.shape[3]
    half, quarter = span // 2, columns // 4
    device = lax.axis_index("blk")
    plane, chip, core = device // 4, device % 4, lax.axis_index("rhs")
    start = panel[0]
    home = lax.rem(start, 4)
    is_a = plane == home
    is_b = plane == lax.rem(start + 1, 4)
    groups = [[4 * z + j for j in range(4)] for z in range(4)]

    def exchange(x):
        return lax.all_to_all(x, "blk", 0, 0, axis_index_groups=groups, tiled=True)

    def permute(x, to):
        return lax.ppermute(x, "blk", [(i, to(i)) for i in range(16)])

    def up(x):
        return permute(x, lambda i: (i + 4) % 16)

    def down(x):
        return permute(x, lambda i: (i + 12) % 16)

    def across(x):
        return permute(x, lambda i: i ^ 8)

    def deal(xs):
        return [permute(x, lambda i, d=d: i ^ d) for d, x in zip((1, 2, 3), xs)]

    def gather(x):
        return deal([x] * 3)

    def swap(x):
        return lax.ppermute(x, "rhs", [(0, 1), (1, 0)])

    slot = start // 4 + jnp.where(is_b & (home == 3), 1, 0)
    keep = lax.rem(plane + start + 1, 2) == 0
    s = scalars([slot, is_a | is_b, start, plane, chip, core, keep, is_a])

    piece = shaped(BF, width, quarter)
    piece32 = shaped(F32, quarter, width)
    matrix = shaped(BF, 4, span, width)
    blocks = shaped(F32, 4, span, quarter)
    blocks16 = shaped(BF, 4, span, quarter)
    own = shaped(F32, span, quarter)

    def small(kernel, name, shapes, arrays, buffers, copies, limit=63):
        return call(
            kernel, name, s, (1,), [HBM] * len(arrays), [whole(*x.shape) for x in shapes], shapes, arrays,
            scratch=[pltpu.VMEM(x.shape, x.dtype) for x in buffers] + [pltpu.SemaphoreType.DMA((copies,))],
            limit=limit,
        )

    (sent,) = sums(s, 0, strips, back_state)
    sent = sent.astype(HF)
    got = permute(sent, lambda i: i ^ 4)

    to_e, to_w = prep(after(s, sent), strips, dinv_rows, fwd_state)
    m = deal(to_e)
    kept, copy = sums(after(s, *to_e), 1, strips, back_state)
    m = after_all(m, kept)
    m_other = [swap(x) for x in m]
    n = deal(to_w)
    hi_p, lo_p, e = small(
        first_kernel, "first", [piece, piece, matrix], (fwd_state, dinv_rows, *m, *m_other), [own, blocks16], 14
    )
    below = up(hi_p)

    pair = (after(kept, hi_p) + got.astype(F32)).astype(HF)
    parts = exchange(pair).reshape(4, quarter, width)

    xp = jnp.where(is_a, hi_p, below)
    xp_far = across(xp)
    n_other = [swap(x) for x in n]
    hi_q, lo = small(
        second_kernel, "second", [piece, piece], (fwd_state, strips, xp, e, *m, *n, *n_other, lo_p),
        [own, blocks16, blocks16, piece, matrix, matrix, piece], 26,
    )
    part = jnp.sum(parts.astype(F32), axis=0)
    part16 = part.astype(HF)

    def last(first):
        source = (first + 1) % 4

        def send(x, *pairs):
            return lax.ppermute(x, "blk", [(4 * a + j, 4 * b + j) for a, b in pairs for j in range(4)])

        def run(x, xp, part):
            far = send(part, (first ^ 2, first), (source ^ 2, source))
            got = [send(x, (source, z)) for z in range(4) if z != source]
            return jnp.where(is_b, x, sum(got)), gather(xp), far.astype(F32)

        return run

    xp = jnp.where(is_a | is_b, xp, xp_far)
    xq, xp_rest, far = lax.switch(home, [last(z) for z in range(4)], hi_q, xp, part16)
    xp_all = [xp] + xp_rest
    xq_all = [xq] + gather(xq)

    y_b, r = small(
        third_kernel, "third", [blocks, piece32], (part, far, e, strips, *n, *n_other),
        [piece32, piece32, matrix, matrix], 13,
    )
    r = down(r)
    lo_own = exchange(after(lo, y_b)).reshape(4, span, quarter)
    state = update(update_one_kernel, after(s, y_b), fwd_state, strips, xp_all)
    y = small(
        fourth_kernel, "fourth", [own] * 4, (part, far, r, e, after(y_b, state, *xq_all)),
        [piece32, piece32, piece32, matrix], 7,
    )
    y = [y[0]] + deal(y[1:])
    fwd_out = update(update_two_kernel, after(s, y[0]), state, strips, xq_all, (*xp_all, lo_own), {1: 0})
    back_out = place(s, copy, y)
    return fwd_out, back_out


def body(panel, strips, dinv_rows, fwd_state, back_state):
    tiles, span, columns = fwd_state.shape
    width = strips.shape[3]
    blocks = lax.axis_size("blk")
    regular = (
        blocks == 16
        and lax.axis_size("rhs") == 2
        and width == 4 * span
        and span % 256 == 0
        and columns % 512 == 0
    )
    chosen = plane_body if regular else plain_body
    return chosen(panel, strips, dinv_rows, fwd_state, back_state)


def solution(mesh):
    return jax.shard_map(
        body,
        mesh=mesh,
        in_specs=(
            P(),
            P(None, None, "blk", None),
            P(None, "blk", None),
            P(None, "blk", "rhs"),
            P(None, "blk", "rhs"),
        ),
        out_specs=(P(None, "blk", "rhs"), P(None, "blk", "rhs")),
        check_vma=False,
    )
```

```python
import functools

import jax
import jax.numpy as jnp
from jax import lax
from jax.experimental import pallas as pl
from jax.experimental.pallas import tpu as pltpu
from jax.sharding import PartitionSpec as P

BF = jnp.bfloat16
HF = jnp.float16
F32 = jnp.float32
SUM_SCALE = 4.0
MIB = 1024 * 1024

NN = (((1,), (0,)), ((), ()))


def mm(a, b, dims):
    return lax.dot_general(a, b, dims, preferred_element_type=F32)


def plain_body(panel, strips, dinv_rows, fwd_state, back_state):
    tiles, span, columns = fwd_state.shape
    width = strips.shape[3]
    per_panel = width // span
    blocks = lax.axis_size("blk")
    device = lax.axis_index("blk")
    start = panel[0]
    slots = jnp.arange(tiles, dtype=jnp.int32)
    block_of = (slots * blocks + device) // per_panel

    def locate(k):
        offset = jnp.mod(device - per_panel * k, blocks)
        holds = offset < per_panel
        local = jnp.clip((per_panel * k + offset) // blocks, 0, tiles - 1)
        return (holds, local, jnp.minimum(offset, per_panel - 1))

    def forward(k, which, state):
        holds, local, offset = locate(k)
        strip = strips[which]
        current = lax.dynamic_index_in_dim(state, local, 0, keepdims=False).astype(BF)
        inv_tile = lax.dynamic_index_in_dim(dinv_rows, local, 0, keepdims=False)
        partial_rows = lax.dot_general(
            inv_tile, current, (((0,), (0,)), ((), ())), preferred_element_type=F32
        )
        partial_rows = jnp.where(holds, partial_rows, 0.0)
        later = (block_of > k)[:, None, None]
        solved = lax.psum(partial_rows, "blk")
        delta = jnp.einsum(
            "atw,wc->atc", strip, solved.astype(BF), preferred_element_type=F32
        )
        state = state - jnp.where(later, delta, 0.0)
        own_tile = lax.dynamic_slice_in_dim(solved, offset * span, span, 0)
        placed = lax.dynamic_update_index_in_dim(state, own_tile, local, 0)
        return jnp.where(holds, placed, state)

    def backward(k, which, state):
        holds, local, offset = locate(k)
        strip = strips[which]
        known = jnp.where((block_of > k)[:, None, None], state, 0.0).astype(BF)
        term = -jnp.einsum("atw,atc->wc", strip, known, preferred_element_type=F32)
        current = lax.dynamic_index_in_dim(state, local, 0, keepdims=False)
        placed_rows = lax.dynamic_update_slice_in_dim(
            jnp.zeros((width, columns), F32), current, offset * span, 0
        )
        term = term + jnp.where(holds, placed_rows, 0.0)
        summed = lax.psum(term, "blk").astype(BF)
        inv_tile = lax.dynamic_index_in_dim(dinv_rows, local, 0, keepdims=False)
        solved_tile = jnp.dot(inv_tile, summed, preferred_element_type=F32)
        placed = lax.dynamic_update_index_in_dim(state, solved_tile, local, 0)
        return jnp.where(holds, placed, state)

    fwd_out = forward(start, 0, fwd_state)
    fwd_out = forward(start + 1, 1, fwd_out)
    back_out = backward(start + 1, 1, back_state)
    back_out = backward(start, 0, back_out)
    return (fwd_out, back_out)


SLOT, OWNS, PANEL, PLANE, CHIP, CORE, KEEP, IS_A = range(8)


def scalars(values):
    lane = lax.broadcasted_iota(jnp.int32, (16,), 0)
    out = jnp.zeros((16,), jnp.int32)
    for i, value in enumerate(values):
        out = jnp.where(lane == i, value.astype(jnp.int32), out)
    return out


def call(kernel, name, s, grid, ins, outs, shapes, arrays, scratch=(), aliases=None, limit=63):
    return pl.pallas_call(
        kernel,
        grid_spec=pltpu.PrefetchScalarGridSpec(
            num_scalar_prefetch=1, grid=grid, in_specs=ins, out_specs=outs, scratch_shapes=list(scratch)
        ),
        out_shape=shapes,
        input_output_aliases=aliases or {},
        compiler_params=pltpu.CompilerParams(vmem_limit_bytes=limit * MIB),
        name=name,
    )(s, *arrays)


HBM = pl.BlockSpec(memory_space=pltpu.HBM)


def whole(*shape):
    return pl.BlockSpec(shape, lambda i, s: (0,) * len(shape), pipeline_mode=pl.Buffered(1))


def shaped(dtype, *shape):
    return jax.ShapeDtypeStruct(shape, dtype)


def later(s, slot):
    return 4 * slot + s[PLANE] > s[PANEL] + 1


def sums_kernel(own, s, strips, state, out_ref, *rest, between=None):
    copies, (bv, wv, sb, sw, so) = rest[:own], rest[own:]
    tiles, span, _ = bv.shape
    which = s[KEEP] if own else 1 - s[KEEP]

    def rows(a):
        return pltpu.make_async_copy(state.at[a], bv.at[a], sb.at[a])

    def strip(a):
        return pltpu.make_async_copy(strips.at[which, a], wv.at[a], sw.at[a])

    def back(a):
        return pltpu.make_async_copy(bv.at[a], copies[0].at[a], so.at[a])

    for a in range(tiles):
        if own:
            rows(a).start()

        @pl.when(later(s, a))
        def _(a=a):
            if not own:
                rows(a).start()
            strip(a).start()

    out_ref[...] = jnp.zeros_like(out_ref)
    if between is not None:
        between()
    for a in range(tiles):
        if own:
            rows(a).wait()
            back(a).start()

        @pl.when(later(s, a))
        def _(a=a):
            if not own:
                rows(a).wait()
            strip(a).wait()
            out_ref[...] += mm((bv[a] * SUM_SCALE).T.astype(BF), wv[a], NN)

    if own:
        @pl.when(s[OWNS] == 1)
        def _():
            at = pl.ds(pl.multiple_of(s[CHIP] * span, span), span)
            out_ref[:, at] = out_ref[:, at] - (bv[s[SLOT]] * SUM_SCALE).T

        for a in range(tiles):
            back(a).wait()


def sent_kernel(s, strips, state, dinv, f, out_ref, *rest):
    outs, (bv, wv, ev, sv, fv, sb, sw, so, sp) = rest[:6], rest[6:]
    half, width = ev.shape
    quarter = (outs[0].shape[1] - width) // 2
    at = pl.ds(pl.multiple_of(s[CORE] * half, half), half)
    copies = begin(
        sp,
        [(f.at[s[SLOT]], fv), (dinv.at[s[SLOT], at, :], ev), (strips.at[0, s[SLOT], at, :], sv)],
    )

    def payloads():
        finish(copies)
        for d in (1, 2, 3):
            at = pl.ds(pl.multiple_of((s[CHIP] ^ d) * quarter, quarter), quarter)
            high, low = split(fv[:, at])
            for out, matrix, part in ((outs[d - 1], ev, high), (outs[d + 2], sv, low)):
                out[:, :width] = matrix[...]
                out[:, width:width + quarter] = part[:half]
                out[:, width + quarter:] = part[half:]

    sums_kernel(False, s, strips, state, out_ref, bv, wv, sb, sw, so, between=payloads)


def sums_and_payloads(s, strips, dinv_rows, fwd_state, back_state):
    tiles, span, columns = back_state.shape
    width = strips.shape[3]
    half, quarter = span // 2, columns // 4
    payload = (half, width + 2 * quarter)
    dma = pltpu.SemaphoreType.DMA
    outs = call(
        sent_kernel, "sums", s, (1,), [HBM] * 4,
        [whole(columns, width)] + [whole(*payload)] * 6,
        [shaped(F32, columns, width)] + [shaped(BF, *payload)] * 6,
        (strips, back_state, dinv_rows, fwd_state),
        scratch=[
            pltpu.VMEM((tiles, span, columns), F32), pltpu.VMEM((tiles, span, width), BF),
            pltpu.VMEM((half, width), BF), pltpu.VMEM((half, width), BF), pltpu.VMEM((span, columns), F32),
            dma((tiles,)), dma((tiles,)), dma((tiles,)), dma((3,)),
        ],
        limit=60,
    )
    return outs[0], outs[1:4], outs[4:]


def sums(s, own, strips, back_state):
    tiles, span, columns = back_state.shape
    width = strips.shape[3]
    return call(
        functools.partial(sums_kernel, own), "sums", s, (1,),
        [HBM] * 2,
        [whole(columns, width)] + [HBM] * own,
        [shaped(F32, columns, width)] + [shaped(F32, *back_state.shape)] * own,
        (strips, back_state),
        scratch=[pltpu.VMEM((tiles, span, columns), F32), pltpu.VMEM((tiles, span, width), BF)]
        + [pltpu.SemaphoreType.DMA((tiles,))] * 3,
        limit=60,
    )


def begin(sems, pairs):
    copies = [pltpu.make_async_copy(a, b, sems.at[i]) for i, (a, b) in enumerate(pairs)]
    for copy in copies:
        copy.start()
    return copies


def finish(copies):
    for copy in copies:
        copy.wait()


def fetch(sems, pairs):
    finish(begin(sems, pairs))


def halves(full, d, mine, other, core):
    half, width = mine.shape[0], full.shape[2]
    return [
        (mine.at[:, :width], full.at[d, pl.ds(pl.multiple_of(core * half, half), half), :]),
        (other.at[:, :width], full.at[d, pl.ds(pl.multiple_of((1 - core) * half, half), half), :]),
    ]


def block(full, d, mine, width):
    half, quarter = mine.shape[0], full.shape[2]
    return [
        (mine.at[:, width:width + quarter], full.at[d, :half, :]),
        (mine.at[:, width + quarter:], full.at[d, half:, :]),
    ]


def own_f(s, f, quarter):
    at = pl.ds(pl.multiple_of(s[CHIP] * quarter, quarter), quarter)
    return f.at[s[SLOT], :, at]


def split(x):
    high = x.astype(BF)
    return high, (x - high.astype(F32)).astype(BF)


def first_kernel(s, f, own, m1, m2, m3, o1, o2, o3, hi, lo, e, fv, hv, sems):
    _, quarter = fv.shape
    width = e.shape[2]
    pairs = [(own_f(s, f, quarter), fv), (own.at[s[SLOT]], e.at[0])]
    for d, mine, other in ((1, m1, o1), (2, m2, o2), (3, m3, o3)):
        pairs += halves(e, d, mine, other, s[CORE]) + block(hv, d, mine, width)
    copies = begin(sems, pairs)
    finish(copies[:2])
    x = mm(fv[...].T.astype(BF), e[0], NN)
    for d in (1, 2, 3):
        finish(copies[4 * d - 2:4 * d + 2])
        x += mm(hv[d].astype(F32).T.astype(BF), e[d], NN)
    hi[...], lo[...] = split(x.T)


def second_kernel(
    s, f, strips, xp, e, m1, m2, m3, n1, n2, n3, o1, o2, o3, lo_a, hi, lo, fv, hv, gv, xv, ev, wv, lv, sems
):
    _, quarter = fv.shape
    width = wv.shape[2]
    pairs = [(xp, xv), (own_f(s, f, quarter), fv), (strips.at[0, s[SLOT]], wv.at[0]), (e.at[0], ev.at[0])]
    for d, first, mine, other in ((1, m1, n1, o1), (2, m2, n2, o2), (3, m3, n3, o3)):
        pairs += halves(wv, d, mine, other, s[CORE])
        pairs += block(hv, d, first, width) + block(gv, d, mine, width) + [(e.at[d], ev.at[d])]
    pairs += [(lo_a, lv)]
    copies = begin(sems, pairs)
    x = jnp.zeros((quarter, width), F32)
    for d in range(4):
        finish(copies[:4] if d == 0 else copies[7 * d - 3:7 * d + 4])
        old = fv[...] if d == 0 else hv[d].astype(F32) + gv[d].astype(F32)
        new = old - mm(wv[d], xv[...], NN)
        x += mm(new.T.astype(BF), ev[d], NN)
    high, low = split(x.T)
    hi[...] = high
    finish(copies[25:])

    @pl.when(s[IS_A] == 1)
    def _():
        lo[...] = lv[...]

    @pl.when(s[IS_A] == 0)
    def _():
        lo[...] = low


def third_kernel(s, part, far, e, strips, n1, n2, n3, o1, o2, o3, y, r, pv, rv, ev, wv, sems):
    pairs = [(part, pv), (far, rv), (e.at[0], ev.at[0]), (strips.at[0, s[SLOT]], wv.at[0])]
    for d, mine, other in ((1, n1, o1), (2, n2, o2), (3, n3, o3)):
        pairs += halves(wv, d, mine, other, s[CORE]) + [(e.at[d], ev.at[d])]
    copies = begin(sems, pairs)
    finish(copies[:2])
    rest = ((pv[...] + rv[...]) * (-1.0 / SUM_SCALE)).T.astype(BF)
    back = jnp.zeros(r.shape, F32)
    for d in range(4):
        finish(copies[2:4] if d == 0 else copies[3 * d + 1:3 * d + 4])
        yq = mm(ev[d], rest, NN)
        y[d] = yq
        back += mm(yq.T.astype(BF), wv[d], NN)
    r[...] = back


def fourth_kernel(s, part, far, r, e, y_b, y0, y1, y2, y3, pv, rv, bv, ev, sems):
    outs = (y0, y1, y2, y3)

    @pl.when(s[IS_A] == 0)
    def _():
        fetch(sems, [(y_b.at[d], y) for d, y in enumerate(outs)])

    @pl.when(s[IS_A] == 1)
    def _():
        copies = begin(sems, [(part, pv), (far, rv), (r, bv)] + [(e.at[d], ev.at[d]) for d in range(4)])
        finish(copies[:3])
        rest = ((pv[...] + rv[...]) * (-1.0 / SUM_SCALE) - bv[...]).T.astype(BF)
        for d, y in enumerate(outs):
            finish(copies[3 + d:4 + d])
            y[...] = mm(ev[d], rest, NN)


def gathered(s, x_full, pieces):
    quarter = pieces[0].shape[1]
    return [
        (x, x_full.at[:, pl.ds(pl.multiple_of((s[CHIP] ^ d) * quarter, quarter), quarter)])
        for d, x in enumerate(pieces)
    ]


def update_one_kernel(s, f, strips, x0, x1, x2, x3, out, fv, wv, xv, sf, sw, so, sx):
    tiles = fv.shape[0]

    def state(a):
        return pltpu.make_async_copy(f.at[a], fv.at[a], sf.at[a])

    def strip(a):
        return pltpu.make_async_copy(strips.at[0, a], wv.at[a], sw.at[a])

    def back(a):
        return pltpu.make_async_copy(fv.at[a], out.at[a], so.at[a])

    x = begin(sx, gathered(s, xv, (x0, x1, x2, x3)))
    for a in range(tiles):
        state(a).start()
        pl.when(later(s, a))(strip(a).start)
    finish(x)
    for a in range(tiles):
        state(a).wait()

        @pl.when(later(s, a))
        def _(a=a):
            strip(a).wait()
            fv[a] = fv[a] - mm(wv[a], xv[...], NN)

        back(a).start()
    for a in range(tiles):
        back(a).wait()


def update_two_kernel(
    s, f, strips, x0, x1, x2, x3, p0, p1, p2, p3, lo, out, fv, wv, xv, sf, sw, so, sx, pv, lv, sp
):
    tiles, span, columns = fv.shape
    quarter = columns // 4
    rows = pl.ds(pl.multiple_of(s[CHIP] * span, span), span)

    def state(a):
        return pltpu.make_async_copy(f.at[a], fv.at[a], sf.at[a])

    def strip(a):
        return pltpu.make_async_copy(strips.at[1, a], wv.at[a], sw.at[a])

    def back(a):
        return pltpu.make_async_copy(fv.at[a], out.at[a], so.at[a])

    x = begin(sx, gathered(s, xv, (x0, x1, x2, x3)))
    for a in range(tiles):
        @pl.when(later(s, a))
        def _(a=a):
            state(a).start()
            strip(a).start()

    own = begin(sp, gathered(s, pv, [p.at[rows, :] for p in (p0, p1, p2, p3)]) + [(lo, lv)])
    finish(x)
    for a in range(tiles):
        @pl.when(later(s, a))
        def _(a=a):
            state(a).wait()
            strip(a).wait()
            fv[a] = fv[a] - mm(wv[a], xv[...], NN)
            back(a).start()

    finish(own)
    for a in range(tiles):
        @pl.when((s[SLOT] == a) & (s[OWNS] == 1))
        def _(a=a):
            solved = jnp.where(s[IS_A] == 1, pv[...].astype(F32), xv[rows, :].astype(F32))
            for q in range(4):
                at = slice(q * quarter, (q + 1) * quarter)
                fv[a, :, at] = solved[:, at] + lv[q].astype(F32)
            back(a).start()
            back(a).wait()

        @pl.when(later(s, a))
        def _(a=a):
            back(a).wait()


def update(kernel, s, state, strips, pieces, own=(), aliases=None):
    tiles, span, columns = state.shape
    width = strips.shape[3]
    dma = pltpu.SemaphoreType.DMA
    more = []
    if own:
        more = [pltpu.VMEM((span, columns), BF), pltpu.VMEM(own[-1].shape, BF), dma((5,))]
    return call(
        kernel, "update", s, (1,), [HBM] * (2 + len(pieces) + len(own)), HBM, shaped(F32, *state.shape),
        (state, strips, *pieces, *own),
        scratch=[
            pltpu.VMEM(state.shape, F32), pltpu.VMEM(strips.shape[1:], BF), pltpu.VMEM((width, columns), BF),
            dma((tiles,)), dma((tiles,)), dma((tiles,)), dma((4,)),
        ] + more,
        aliases=aliases,
    )


def place_kernel(s, copy, y0, y1, y2, y3, out, tile, sems):
    @pl.when(s[OWNS] == 1)
    def _():
        fetch(sems, gathered(s, tile, (y0, y1, y2, y3)))
        fetch(sems, [(tile, out.at[s[SLOT]])])


def place(s, copy, pieces):
    _, span, columns = copy.shape
    return call(
        place_kernel, "place", s, (1,), [HBM] * 5, HBM, shaped(F32, *copy.shape), (copy, *pieces),
        scratch=[pltpu.VMEM((span, columns), F32), pltpu.SemaphoreType.DMA((4,))],
        aliases={1: 0}, limit=8,
    )


def after(x, *waits):
    return lax.optimization_barrier((x,) + waits)[0]


def after_all(xs, *waits):
    return lax.optimization_barrier(tuple(xs) + waits)[:len(xs)]


def plane_body(panel, strips, dinv_rows, fwd_state, back_state):
    tiles, span, columns = fwd_state.shape
    width = strips.shape[3]
    half, quarter = span // 2, columns // 4
    device = lax.axis_index("blk")
    plane, chip, core = device // 4, device % 4, lax.axis_index("rhs")
    start = panel[0]
    home = lax.rem(start, 4)
    is_a = plane == home
    is_b = plane == lax.rem(start + 1, 4)
    groups = [[4 * z + j for j in range(4)] for z in range(4)]

    def exchange(x):
        return lax.all_to_all(x, "blk", 0, 0, axis_index_groups=groups, tiled=True)

    def permute(x, to):
        return lax.ppermute(x, "blk", [(i, to(i)) for i in range(16)])

    def up(x):
        return permute(x, lambda i: (i + 4) % 16)

    def down(x):
        return permute(x, lambda i: (i + 12) % 16)

    def across(x):
        return permute(x, lambda i: i ^ 8)

    def deal(xs):
        return [permute(x, lambda i, d=d: i ^ d) for d, x in zip((1, 2, 3), xs)]

    def gather(x):
        return deal([x] * 3)

    def swap(x):
        return lax.ppermute(x, "rhs", [(0, 1), (1, 0)])

    slot = start // 4 + jnp.where(is_b & (home == 3), 1, 0)
    keep = lax.rem(plane + start + 1, 2) == 0
    s = scalars([slot, is_a | is_b, start, plane, chip, core, keep, is_a])

    piece = shaped(BF, width, quarter)
    piece32 = shaped(F32, quarter, width)
    matrix = shaped(BF, 4, span, width)
    blocks = shaped(F32, 4, span, quarter)
    blocks16 = shaped(BF, 4, span, quarter)
    own = shaped(F32, span, quarter)

    def small(kernel, name, shapes, arrays, buffers, copies, limit=63):
        return call(
            kernel, name, s, (1,), [HBM] * len(arrays), [whole(*x.shape) for x in shapes], shapes, arrays,
            scratch=[pltpu.VMEM(x.shape, x.dtype) for x in buffers] + [pltpu.SemaphoreType.DMA((copies,))],
            limit=limit,
        )

    sent, to_e, to_w = sums_and_payloads(s, strips, dinv_rows, fwd_state, back_state)
    sent = sent.astype(HF)
    got = permute(sent, lambda i: i ^ 4)
    m = deal(to_e)
    kept, copy = sums(after(s, *to_e), 1, strips, back_state)
    m = after_all(m, kept)
    m_other = [swap(x) for x in m]
    n = deal(to_w)
    hi_p, lo_p, e = small(
        first_kernel, "first", [piece, piece, matrix], (fwd_state, dinv_rows, *m, *m_other), [own, blocks16], 14
    )
    below = up(hi_p)

    pair = (after(kept, hi_p, n[0]) + got.astype(F32)).astype(HF)
    parts = exchange(pair).reshape(4, quarter, width)

    xp = jnp.where(is_a, hi_p, below)
    xp_far = across(xp)
    n_other = [swap(x) for x in n]
    hi_q, lo = small(
        second_kernel, "second", [piece, piece], (fwd_state, strips, xp, e, *m, *n, *n_other, lo_p),
        [own, blocks16, blocks16, piece, matrix, matrix, piece], 26,
    )
    part = jnp.sum(parts.astype(F32), axis=0)
    part16 = part.astype(HF)

    def last(first):
        source = (first + 1) % 4

        def send(x, *pairs):
            return lax.ppermute(x, "blk", [(4 * a + j, 4 * b + j) for a, b in pairs for j in range(4)])

        def run(x, xp, part):
            far = send(part, (first ^ 2, first), (source ^ 2, source))
            got = [send(x, (source, z)) for z in range(4) if z != source]
            return jnp.where(is_b, x, sum(got)), gather(xp), far.astype(F32)

        return run

    xp = jnp.where(is_a | is_b, xp, xp_far)
    xq, xp_rest, far = lax.switch(home, [last(z) for z in range(4)], hi_q, xp, part16)
    xp_all = [xp] + xp_rest
    xq_all = [xq] + gather(xq)

    y_b, r = small(
        third_kernel, "third", [blocks, piece32], (part, far, e, strips, *n, *n_other),
        [piece32, piece32, matrix, matrix], 13,
    )
    r = down(r)
    lo_own = exchange(after(lo, y_b)).reshape(4, span, quarter)
    state = update(update_one_kernel, after(s, y_b), fwd_state, strips, xp_all)
    y = small(
        fourth_kernel, "fourth", [own] * 4, (part, far, r, e, after(y_b, state, *xq_all)),
        [piece32, piece32, piece32, matrix], 7,
    )
    y = [y[0]] + deal(y[1:])
    fwd_out = update(update_two_kernel, after(s, y[0]), state, strips, xq_all, (*xp_all, lo_own), {1: 0})
    back_out = place(s, copy, y)
    return fwd_out, back_out


def body(panel, strips, dinv_rows, fwd_state, back_state):
    tiles, span, columns = fwd_state.shape
    width = strips.shape[3]
    blocks = lax.axis_size("blk")
    regular = (
        blocks == 16
        and lax.axis_size("rhs") == 2
        and width == 4 * span
        and span % 256 == 0
        and columns % 512 == 0
    )
    chosen = plane_body if regular else plain_body
    return chosen(panel, strips, dinv_rows, fwd_state, back_state)


def solution(mesh):
    return jax.shard_map(
        body,
        mesh=mesh,
        in_specs=(
            P(),
            P(None, None, "blk", None),
            P(None, "blk", None),
            P(None, "blk", "rhs"),
            P(None, "blk", "rhs"),
        ),
        out_specs=(P(None, "blk", "rhs"), P(None, "blk", "rhs")),
        check_vma=False,
    )
```

```python
import functools

import jax
import jax.numpy as jnp
from jax import lax
from jax.experimental import pallas as pl
from jax.experimental.pallas import tpu as pltpu
from jax.sharding import PartitionSpec as P

BF = jnp.bfloat16
HF = jnp.float16
F32 = jnp.float32
SUM_SCALE = 4.0
MIB = 1024 * 1024

NN = (((1,), (0,)), ((), ()))


def mm(a, b, dims):
    return lax.dot_general(a, b, dims, preferred_element_type=F32)


def plain_body(panel, strips, dinv_rows, fwd_state, back_state):
    tiles, span, columns = fwd_state.shape
    width = strips.shape[3]
    per_panel = width // span
    blocks = lax.axis_size("blk")
    device = lax.axis_index("blk")
    start = panel[0]
    slots = jnp.arange(tiles, dtype=jnp.int32)
    block_of = (slots * blocks + device) // per_panel

    def locate(k):
        offset = jnp.mod(device - per_panel * k, blocks)
        holds = offset < per_panel
        local = jnp.clip((per_panel * k + offset) // blocks, 0, tiles - 1)
        return (holds, local, jnp.minimum(offset, per_panel - 1))

    def forward(k, which, state):
        holds, local, offset = locate(k)
        strip = strips[which]
        current = lax.dynamic_index_in_dim(state, local, 0, keepdims=False).astype(BF)
        inv_tile = lax.dynamic_index_in_dim(dinv_rows, local, 0, keepdims=False)
        partial_rows = lax.dot_general(
            inv_tile, current, (((0,), (0,)), ((), ())), preferred_element_type=F32
        )
        partial_rows = jnp.where(holds, partial_rows, 0.0)
        later = (block_of > k)[:, None, None]
        solved = lax.psum(partial_rows, "blk")
        delta = jnp.einsum(
            "atw,wc->atc", strip, solved.astype(BF), preferred_element_type=F32
        )
        state = state - jnp.where(later, delta, 0.0)
        own_tile = lax.dynamic_slice_in_dim(solved, offset * span, span, 0)
        placed = lax.dynamic_update_index_in_dim(state, own_tile, local, 0)
        return jnp.where(holds, placed, state)

    def backward(k, which, state):
        holds, local, offset = locate(k)
        strip = strips[which]
        known = jnp.where((block_of > k)[:, None, None], state, 0.0).astype(BF)
        term = -jnp.einsum("atw,atc->wc", strip, known, preferred_element_type=F32)
        current = lax.dynamic_index_in_dim(state, local, 0, keepdims=False)
        placed_rows = lax.dynamic_update_slice_in_dim(
            jnp.zeros((width, columns), F32), current, offset * span, 0
        )
        term = term + jnp.where(holds, placed_rows, 0.0)
        summed = lax.psum(term, "blk").astype(BF)
        inv_tile = lax.dynamic_index_in_dim(dinv_rows, local, 0, keepdims=False)
        solved_tile = jnp.dot(inv_tile, summed, preferred_element_type=F32)
        placed = lax.dynamic_update_index_in_dim(state, solved_tile, local, 0)
        return jnp.where(holds, placed, state)

    fwd_out = forward(start, 0, fwd_state)
    fwd_out = forward(start + 1, 1, fwd_out)
    back_out = backward(start + 1, 1, back_state)
    back_out = backward(start, 0, back_out)
    return (fwd_out, back_out)


SLOT, OWNS, PANEL, PLANE, CHIP, CORE, KEEP, IS_A = range(8)


def scalars(values):
    lane = lax.broadcasted_iota(jnp.int32, (16,), 0)
    out = jnp.zeros((16,), jnp.int32)
    for i, value in enumerate(values):
        out = jnp.where(lane == i, value.astype(jnp.int32), out)
    return out


def call(kernel, name, s, grid, ins, outs, shapes, arrays, scratch=(), aliases=None, limit=63):
    return pl.pallas_call(
        kernel,
        grid_spec=pltpu.PrefetchScalarGridSpec(
            num_scalar_prefetch=1, grid=grid, in_specs=ins, out_specs=outs, scratch_shapes=list(scratch)
        ),
        out_shape=shapes,
        input_output_aliases=aliases or {},
        compiler_params=pltpu.CompilerParams(vmem_limit_bytes=limit * MIB),
        name=name,
    )(s, *arrays)


HBM = pl.BlockSpec(memory_space=pltpu.HBM)


def whole(*shape):
    return pl.BlockSpec(shape, lambda i, s: (0,) * len(shape), pipeline_mode=pl.Buffered(1))


def shaped(dtype, *shape):
    return jax.ShapeDtypeStruct(shape, dtype)


def later(s, slot):
    return 4 * slot + s[PLANE] > s[PANEL] + 1


def sums_kernel(own, s, strips, state, out_ref, *rest, between=None):
    copies, (bv, wv, sb, sw, so) = rest[:own], rest[own:]
    tiles, span, _ = bv.shape
    which = s[KEEP] if own else 1 - s[KEEP]

    def rows(a):
        return pltpu.make_async_copy(state.at[a], bv.at[a], sb.at[a])

    def strip(a):
        return pltpu.make_async_copy(strips.at[which, a], wv.at[a], sw.at[a])

    def back(a):
        return pltpu.make_async_copy(bv.at[a], copies[0].at[a], so.at[a])

    for a in range(tiles):
        if own:
            rows(a).start()

        @pl.when(later(s, a))
        def _(a=a):
            if not own:
                rows(a).start()
            strip(a).start()

    out_ref[...] = jnp.zeros_like(out_ref)
    if between is not None:
        between()
    for a in range(tiles):
        if own:
            rows(a).wait()
            back(a).start()

        @pl.when(later(s, a))
        def _(a=a):
            if not own:
                rows(a).wait()
            strip(a).wait()
            out_ref[...] += mm((bv[a] * SUM_SCALE).T.astype(BF), wv[a], NN)

    if own:
        @pl.when(s[OWNS] == 1)
        def _():
            at = pl.ds(pl.multiple_of(s[CHIP] * span, span), span)
            out_ref[:, at] = out_ref[:, at] - (bv[s[SLOT]] * SUM_SCALE).T

        for a in range(tiles):
            back(a).wait()


def sent_kernel(s, strips, state, dinv, f, out_ref, *rest):
    outs, (bv, wv, ev, sv, fv, sb, sw, so, sp) = rest[:6], rest[6:]
    half, width = ev.shape
    quarter = (outs[0].shape[1] - width) // 2
    at = pl.ds(pl.multiple_of(s[CORE] * half, half), half)
    copies = begin(
        sp,
        [(f.at[s[SLOT]], fv), (dinv.at[s[SLOT], at, :], ev), (strips.at[0, s[SLOT], at, :], sv)],
    )

    def payloads():
        finish(copies)
        for d in (1, 2, 3):
            at = pl.ds(pl.multiple_of((s[CHIP] ^ d) * quarter, quarter), quarter)
            high, low = split(fv[:, at])
            for out, matrix, part in ((outs[d - 1], ev, high), (outs[d + 2], sv, low)):
                out[:, :width] = matrix[...]
                out[:, width:width + quarter] = part[:half]
                out[:, width + quarter:] = part[half:]

    sums_kernel(False, s, strips, state, out_ref, bv, wv, sb, sw, so, between=payloads)


def sums_and_payloads(s, strips, dinv_rows, fwd_state, back_state):
    tiles, span, columns = back_state.shape
    width = strips.shape[3]
    half, quarter = span // 2, columns // 4
    payload = (half, width + 2 * quarter)
    dma = pltpu.SemaphoreType.DMA
    outs = call(
        sent_kernel, "sums", s, (1,), [HBM] * 4,
        [whole(columns, width)] + [whole(*payload)] * 6,
        [shaped(F32, columns, width)] + [shaped(BF, *payload)] * 6,
        (strips, back_state, dinv_rows, fwd_state),
        scratch=[
            pltpu.VMEM((tiles, span, columns), F32), pltpu.VMEM((tiles, span, width), BF),
            pltpu.VMEM((half, width), BF), pltpu.VMEM((half, width), BF), pltpu.VMEM((span, columns), F32),
            dma((tiles,)), dma((tiles,)), dma((tiles,)), dma((3,)),
        ],
        limit=60,
    )
    return outs[0], outs[1:4], outs[4:]


def sums(s, own, strips, back_state):
    tiles, span, columns = back_state.shape
    width = strips.shape[3]
    return call(
        functools.partial(sums_kernel, own), "sums", s, (1,),
        [HBM] * 2,
        [whole(columns, width)] + [HBM] * own,
        [shaped(F32, columns, width)] + [shaped(F32, *back_state.shape)] * own,
        (strips, back_state),
        scratch=[pltpu.VMEM((tiles, span, columns), F32), pltpu.VMEM((tiles, span, width), BF)]
        + [pltpu.SemaphoreType.DMA((tiles,))] * 3,
        limit=60,
    )


def begin(sems, pairs):
    copies = [pltpu.make_async_copy(a, b, sems.at[i]) for i, (a, b) in enumerate(pairs)]
    for copy in copies:
        copy.start()
    return copies


def finish(copies):
    for copy in copies:
        copy.wait()


def fetch(sems, pairs):
    finish(begin(sems, pairs))


def halves(full, d, mine, other, core):
    half, width = mine.shape[0], full.shape[2]
    return [
        (mine.at[:, :width], full.at[d, pl.ds(pl.multiple_of(core * half, half), half), :]),
        (other.at[:, :width], full.at[d, pl.ds(pl.multiple_of((1 - core) * half, half), half), :]),
    ]


def block(full, d, mine, width):
    half, quarter = mine.shape[0], full.shape[2]
    return [
        (mine.at[:, width:width + quarter], full.at[d, :half, :]),
        (mine.at[:, width + quarter:], full.at[d, half:, :]),
    ]


def own_f(s, f, quarter):
    at = pl.ds(pl.multiple_of(s[CHIP] * quarter, quarter), quarter)
    return f.at[s[SLOT], :, at]


def split(x):
    high = x.astype(BF)
    return high, (x - high.astype(F32)).astype(BF)


def first_kernel(s, f, own, m1, m2, m3, o1, o2, o3, hi, lo, e, fv, hv, sems):
    _, quarter = fv.shape
    width = e.shape[2]
    pairs = [(own_f(s, f, quarter), fv), (own.at[s[SLOT]], e.at[0])]
    for d, mine, other in ((1, m1, o1), (2, m2, o2), (3, m3, o3)):
        pairs += halves(e, d, mine, other, s[CORE]) + block(hv, d, mine, width)
    copies = begin(sems, pairs)
    finish(copies[:2])
    x = mm(fv[...].T.astype(BF), e[0], NN)
    for d in (1, 2, 3):
        finish(copies[4 * d - 2:4 * d + 2])
        x += mm(hv[d].astype(F32).T.astype(BF), e[d], NN)
    hi[...], lo[...] = split(x.T)


def second_kernel(
    s, f, strips, xp, e, m1, m2, m3, n1, n2, n3, o1, o2, o3, lo_a, hi, lo, fv, hv, gv, xv, ev, wv, lv, sems
):
    _, quarter = fv.shape
    width = wv.shape[2]
    pairs = [(xp, xv), (own_f(s, f, quarter), fv), (strips.at[0, s[SLOT]], wv.at[0]), (e.at[0], ev.at[0])]
    for d, first, mine, other in ((1, m1, n1, o1), (2, m2, n2, o2), (3, m3, n3, o3)):
        pairs += halves(wv, d, mine, other, s[CORE])
        pairs += block(hv, d, first, width) + block(gv, d, mine, width) + [(e.at[d], ev.at[d])]
    pairs += [(lo_a, lv)]
    copies = begin(sems, pairs)
    x = jnp.zeros((quarter, width), F32)
    for d in range(4):
        finish(copies[:4] if d == 0 else copies[7 * d - 3:7 * d + 4])
        old = fv[...] if d == 0 else hv[d].astype(F32) + gv[d].astype(F32)
        new = old - mm(wv[d], xv[...], NN)
        x += mm(new.T.astype(BF), ev[d], NN)
    high, low = split(x.T)
    hi[...] = high
    finish(copies[25:])

    @pl.when(s[IS_A] == 1)
    def _():
        lo[...] = lv[...]

    @pl.when(s[IS_A] == 0)
    def _():
        lo[...] = low


def third_kernel(s, part, far, e, strips, n1, n2, n3, o1, o2, o3, y, r, pv, rv, ev, wv, sems):
    pairs = [(part, pv), (far, rv), (e.at[0], ev.at[0]), (strips.at[0, s[SLOT]], wv.at[0])]
    for d, mine, other in ((1, n1, o1), (2, n2, o2), (3, n3, o3)):
        pairs += halves(wv, d, mine, other, s[CORE]) + [(e.at[d], ev.at[d])]
    copies = begin(sems, pairs)
    finish(copies[:2])
    rest = ((pv[...] + rv[...]) * (-1.0 / SUM_SCALE)).T.astype(BF)
    back = jnp.zeros(r.shape, F32)
    for d in range(4):
        finish(copies[2:4] if d == 0 else copies[3 * d + 1:3 * d + 4])
        yq = mm(ev[d], rest, NN)
        y[d] = yq
        back += mm(yq.T.astype(BF), wv[d], NN)
    r[...] = back


def fourth_kernel(s, part, far, r, e, y_b, y0, y1, y2, y3, pv, rv, bv, ev, sems):
    outs = (y0, y1, y2, y3)

    @pl.when(s[IS_A] == 0)
    def _():
        fetch(sems, [(y_b.at[d], y) for d, y in enumerate(outs)])

    @pl.when(s[IS_A] == 1)
    def _():
        copies = begin(sems, [(part, pv), (far, rv), (r, bv)] + [(e.at[d], ev.at[d]) for d in range(4)])
        finish(copies[:3])
        rest = ((pv[...] + rv[...]) * (-1.0 / SUM_SCALE) - bv[...]).T.astype(BF)
        for d, y in enumerate(outs):
            finish(copies[3 + d:4 + d])
            y[...] = mm(ev[d], rest, NN)


def gathered(s, x_full, pieces):
    quarter = pieces[0].shape[1]
    return [
        (x, x_full.at[:, pl.ds(pl.multiple_of((s[CHIP] ^ d) * quarter, quarter), quarter)])
        for d, x in enumerate(pieces)
    ]


def update_one_kernel(s, f, strips, x0, x1, x2, x3, out, fv, wv, xv, sf, sw, so, sx):
    tiles = fv.shape[0]

    def state(a):
        return pltpu.make_async_copy(f.at[a], fv.at[a], sf.at[a])

    def strip(a):
        return pltpu.make_async_copy(strips.at[0, a], wv.at[a], sw.at[a])

    def back(a):
        return pltpu.make_async_copy(fv.at[a], out.at[a], so.at[a])

    x = begin(sx, gathered(s, xv, (x0, x1, x2, x3)))
    for a in range(tiles):
        state(a).start()
        pl.when(later(s, a))(strip(a).start)
    finish(x)
    for a in range(tiles):
        state(a).wait()

        @pl.when(later(s, a))
        def _(a=a):
            strip(a).wait()
            fv[a] = fv[a] - mm(wv[a], xv[...], NN)

        back(a).start()
    for a in range(tiles):
        back(a).wait()


def update_two_kernel(
    s, f, strips, x0, x1, x2, x3, p0, p1, p2, p3, lo, out, fv, wv, xv, sf, sw, so, sx, pv, lv, sp
):
    tiles, span, columns = fv.shape
    quarter = columns // 4
    rows = pl.ds(pl.multiple_of(s[CHIP] * span, span), span)

    def state(a):
        return pltpu.make_async_copy(f.at[a], fv.at[a], sf.at[a])

    def strip(a):
        return pltpu.make_async_copy(strips.at[1, a], wv.at[a], sw.at[a])

    def back(a):
        return pltpu.make_async_copy(fv.at[a], out.at[a], so.at[a])

    x = begin(sx, gathered(s, xv, (x0, x1, x2, x3)))
    for a in range(tiles):
        @pl.when(later(s, a))
        def _(a=a):
            state(a).start()
            strip(a).start()

    own = begin(sp, gathered(s, pv, [p.at[rows, :] for p in (p0, p1, p2, p3)]) + [(lo, lv)])
    finish(x)
    for a in range(tiles):
        @pl.when(later(s, a))
        def _(a=a):
            state(a).wait()
            strip(a).wait()
            fv[a] = fv[a] - mm(wv[a], xv[...], NN)
            back(a).start()

    finish(own)
    for a in range(tiles):
        @pl.when((s[SLOT] == a) & (s[OWNS] == 1))
        def _(a=a):
            solved = jnp.where(s[IS_A] == 1, pv[...].astype(F32), xv[rows, :].astype(F32))
            for q in range(4):
                at = slice(q * quarter, (q + 1) * quarter)
                fv[a, :, at] = solved[:, at] + lv[q].astype(F32)
            back(a).start()
            back(a).wait()

        @pl.when(later(s, a))
        def _(a=a):
            back(a).wait()


def update(kernel, s, state, strips, pieces, own=(), aliases=None):
    tiles, span, columns = state.shape
    width = strips.shape[3]
    dma = pltpu.SemaphoreType.DMA
    more = []
    if own:
        more = [pltpu.VMEM((span, columns), BF), pltpu.VMEM(own[-1].shape, BF), dma((5,))]
    return call(
        kernel, "update", s, (1,), [HBM] * (2 + len(pieces) + len(own)), HBM, shaped(F32, *state.shape),
        (state, strips, *pieces, *own),
        scratch=[
            pltpu.VMEM(state.shape, F32), pltpu.VMEM(strips.shape[1:], BF), pltpu.VMEM((width, columns), BF),
            dma((tiles,)), dma((tiles,)), dma((tiles,)), dma((4,)),
        ] + more,
        aliases=aliases,
    )


def place_kernel(s, copy, y0, y1, y2, y3, out, tile, sems):
    @pl.when(s[OWNS] == 1)
    def _():
        fetch(sems, gathered(s, tile, (y0, y1, y2, y3)))
        fetch(sems, [(tile, out.at[s[SLOT]])])


def place(s, copy, pieces):
    _, span, columns = copy.shape
    return call(
        place_kernel, "place", s, (1,), [HBM] * 5, HBM, shaped(F32, *copy.shape), (copy, *pieces),
        scratch=[pltpu.VMEM((span, columns), F32), pltpu.SemaphoreType.DMA((4,))],
        aliases={1: 0}, limit=8,
    )


def after(x, *waits):
    return lax.optimization_barrier((x,) + waits)[0]


def after_all(xs, *waits):
    return lax.optimization_barrier(tuple(xs) + waits)[:len(xs)]


def plane_body(panel, strips, dinv_rows, fwd_state, back_state):
    tiles, span, columns = fwd_state.shape
    width = strips.shape[3]
    half, quarter = span // 2, columns // 4
    device = lax.axis_index("blk")
    plane, chip, core = device // 4, device % 4, lax.axis_index("rhs")
    start = panel[0]
    home = lax.rem(start, 4)
    is_a = plane == home
    is_b = plane == lax.rem(start + 1, 4)
    groups = [[4 * z + j for j in range(4)] for z in range(4)]

    def exchange(x):
        return lax.all_to_all(x, "blk", 0, 0, axis_index_groups=groups, tiled=True)

    def permute(x, to):
        return lax.ppermute(x, "blk", [(i, to(i)) for i in range(16)])

    def up(x):
        return permute(x, lambda i: (i + 4) % 16)

    def down(x):
        return permute(x, lambda i: (i + 12) % 16)

    def across(x):
        return permute(x, lambda i: i ^ 8)

    def deal(xs):
        return [permute(x, lambda i, d=d: i ^ d) for d, x in zip((1, 2, 3), xs)]

    def gather(x):
        return deal([x] * 3)

    def swap(x):
        return lax.ppermute(x, "rhs", [(0, 1), (1, 0)])

    slot = start // 4 + jnp.where(is_b & (home == 3), 1, 0)
    keep = lax.rem(plane + start + 1, 2) == 0
    s = scalars([slot, is_a | is_b, start, plane, chip, core, keep, is_a])

    piece = shaped(BF, width, quarter)
    piece32 = shaped(F32, quarter, width)
    matrix = shaped(BF, 4, span, width)
    blocks = shaped(F32, 4, span, quarter)
    blocks16 = shaped(BF, 4, span, quarter)
    own = shaped(F32, span, quarter)

    def small(kernel, name, shapes, arrays, buffers, copies, limit=63):
        return call(
            kernel, name, s, (1,), [HBM] * len(arrays), [whole(*x.shape) for x in shapes], shapes, arrays,
            scratch=[pltpu.VMEM(x.shape, x.dtype) for x in buffers] + [pltpu.SemaphoreType.DMA((copies,))],
            limit=limit,
        )

    sent, to_e, to_w = sums_and_payloads(s, strips, dinv_rows, fwd_state, back_state)
    sent = sent.astype(HF)
    got = permute(sent, lambda i: i ^ 4)
    m = deal(to_e)
    kept, copy = sums(after(s, *to_e), 1, strips, back_state)
    m = after_all(m, kept)
    m_other = [swap(x) for x in m]
    n = deal(to_w)
    hi_p, lo_p, e = small(
        first_kernel, "first", [piece, piece, matrix], (fwd_state, dinv_rows, *m, *m_other), [own, blocks16], 14
    )
    below = up(hi_p)

    pair = (after(kept, hi_p, n[0]) + got.astype(F32)).astype(HF)
    parts = exchange(pair).reshape(4, quarter, width)

    xp = jnp.where(is_a, hi_p, below)
    xp_far = across(xp)
    n_other = [swap(x) for x in n]
    hi_q, lo = small(
        second_kernel, "second", [piece, piece], (fwd_state, strips, xp, e, *m, *n, *n_other, lo_p),
        [own, blocks16, blocks16, piece, matrix, matrix, piece], 26,
    )
    part = jnp.sum(parts.astype(F32), axis=0)
    part16 = part.astype(HF)

    def last(first):
        source = (first + 1) % 4

        def send(x, *pairs):
            return lax.ppermute(x, "blk", [(4 * a + j, 4 * b + j) for a, b in pairs for j in range(4)])

        def run(x, xp, part, lo):
            far = send(part, (first ^ 2, first), (source ^ 2, source))
            got = [send(x, (source, z)) for z in range(4) if z != source]
            own = exchange(lo).reshape(4, span, quarter)
            return jnp.where(is_b, x, sum(got)), gather(xp), far.astype(F32), own

        return run

    xp = jnp.where(is_a | is_b, xp, xp_far)
    xq, xp_rest, far, lo_own = lax.switch(home, [last(z) for z in range(4)], hi_q, xp, part16, lo)
    xp_all = [xp] + xp_rest
    xq_all = [xq] + gather(xq)

    y_b, r = small(
        third_kernel, "third", [blocks, piece32], (part, far, e, strips, *n, *n_other),
        [piece32, piece32, matrix, matrix], 13,
    )
    r = down(r)
    state = update(update_one_kernel, after(s, y_b), fwd_state, strips, xp_all)
    y = small(
        fourth_kernel, "fourth", [own] * 4, (part, far, r, e, after(y_b, state, *xq_all)),
        [piece32, piece32, piece32, matrix], 7,
    )
    y = [y[0]] + deal(y[1:])
    fwd_out = update(update_two_kernel, after(s, y[0]), state, strips, xq_all, (*xp_all, lo_own), {1: 0})
    back_out = place(s, copy, y)
    return fwd_out, back_out


def body(panel, strips, dinv_rows, fwd_state, back_state):
    tiles, span, columns = fwd_state.shape
    width = strips.shape[3]
    blocks = lax.axis_size("blk")
    regular = (
        blocks == 16
        and lax.axis_size("rhs") == 2
        and width == 4 * span
        and span % 256 == 0
        and columns % 512 == 0
    )
    chosen = plane_body if regular else plain_body
    return chosen(panel, strips, dinv_rows, fwd_state, back_state)


def solution(mesh):
    return jax.shard_map(
        body,
        mesh=mesh,
        in_specs=(
            P(),
            P(None, None, "blk", None),
            P(None, "blk", None),
            P(None, "blk", "rhs"),
            P(None, "blk", "rhs"),
        ),
        out_specs=(P(None, "blk", "rhs"), P(None, "blk", "rhs")),
        check_vma=False,
    )
```
